256 devices in a mesh: dp: 64 (over x, y, z_lo, core), tensor: 4 (over z_hi).
Axes of the slice: x: 4, y: 4, z: 8 (z_hi: 4, z_lo: 2; z = z_hi * 2 + z_lo), core: 2. Of those that a mesh axis runs over, the one named last changes fastest.
Arguments:
- activations: bfloat16 [49152, 8192], P('dp'), may hold values from -48 to 48
- cotangent: bfloat16 [49152, 1024], P('dp', 'tensor'), may hold values from -0.375 to 0.375
- sampled_rows: int32 [4096], P('dp'), may hold values from 0 to 767
- block_owner: int32 [32], replicated, may hold values from 0 to 63, as said below
Outputs:
- natural_step: float32 [8192, 1024], P('dp', 'tensor')
- owner_block_inverses: float32 [64, 256, 256], P('dp')
The draws below stay inside these ranges and needn't reach their ends.
Inputs may be any that keep to these rules, and one draw needn't show every extreme that they name: `block_owner`: each index of dp owns either no block or exactly 1 block; block 0 is owned by index 32.
All inputs are finite; a program needn't handle non-finite values. Where the reference program divides by a largest or mean magnitude, that divisor is 1e-20 or more.
Results may differ from the reference program's by a relative error of at most 0.0003.
Values may be sent and summed in bfloat16 or wider, within the bound.
A program may use at most 128 MiB of HBM per device.

```python
import math
import jax
import jax.numpy as jnp
from jax import lax

D = 8192
KVW = 1024
TOK_DEV = 768
S_DEV = 64
FACTOR_BLOCK = 256
ITERS = 10
TOKENS = 49152
SAMPLES = 4096
NBLK = 32
GW = 256
CAP = 1
SLOT_TOTAL = 64
N_DP = 64
N_TENSOR = 4


def log_spread(key, count, low_end, high_end):
    uniform_unit = jax.random.uniform(key, (count,), jnp.float32)
    return low_end * jnp.exp(uniform_unit * math.log(high_end / low_end))


def scaled_field(key, row_total, column_total):
    subkeys = jax.random.split(key, 3)
    starting_values = jnp.clip(jax.random.normal(subkeys[0], (row_total, column_total), jnp.float32), -4.0, 4.0)
    row_scale = log_spread(subkeys[1], row_total, 0.3, 3.0)
    column_scale = log_spread(subkeys[2], column_total, 0.3, 3.0)
    return starting_values * row_scale[:, None] * column_scale[None, :]


def draw_activations(key, part):
    return scaled_field(jax.random.fold_in(key, 11), TOKENS, D).astype(jnp.bfloat16)


def draw_cotangent(key, part):
    return (scaled_field(jax.random.fold_in(key, 23), TOKENS, KVW) / 128.0).astype(jnp.bfloat16)


def draw_block_owner(key, part):
    key_blocks, key_devices = jax.random.split(jax.random.fold_in(key, 37))
    block_order = jax.random.permutation(key_blocks, NBLK)
    positions = jnp.argsort(block_order)
    mapping = jax.random.permutation(key_devices, N_DP).astype(jnp.int32)
    target = (positions[0] % N_DP).astype(jnp.int32)
    half_index = jnp.int32(N_DP // 2)
    current = jnp.take(mapping, target)
    device_ids = jnp.arange(N_DP, dtype=jnp.int32)
    swapped = jnp.where(mapping == half_index, current, mapping)
    swapped = jnp.where(device_ids == target, half_index, swapped)
    return jnp.take(swapped, positions % N_DP).astype(jnp.int32)


def plant(drawn, stream_key, smallest, largest):
    longest = drawn.shape.index(max(drawn.shape))
    spots = []
    for shift in (0, 1):
        where = [jax.random.randint(jax.random.fold_in(stream_key, axis), (), 0, length) for axis, length in enumerate(drawn.shape)]
        where[longest] = (where[longest] + shift) % drawn.shape[longest]
        spots.append(tuple(where))
    return drawn.at[spots[0]].set(smallest).at[spots[1]].set(largest)


def setup_inputs(seed: int = 0) -> dict:
    seeds = jax.random.split(jax.random.key(seed), 5)
    return {
        "activations": draw_activations(jax.random.fold_in(seeds[4], 71), 0),
        "cotangent": draw_cotangent(jax.random.fold_in(seeds[4], 71), 0),
        "sampled_rows": plant(jax.random.randint(seeds[2], (SAMPLES,), 0, TOK_DEV), jax.random.fold_in(seeds[2], 1), 0, TOK_DEV - 1).astype(jnp.int32),
        "block_owner": draw_block_owner(jax.random.fold_in(seeds[4], 71), 0),
    }


DAMPING = 0.05
precise_mode = lax.Precision.HIGHEST


def newton_inverse(matrix):
    extent = matrix.shape[-1]
    identity = jnp.eye(extent, dtype=jnp.float32)
    row_bound = jnp.max(jnp.sum(jnp.abs(matrix), axis=2), axis=1)
    initial = identity[None, :, :] / row_bound[:, None, None]

    def advance(turn_index, current):
        product = jnp.einsum("nij,njk->nik", matrix, current, precision=precise_mode)
        return jnp.einsum("nij,njk->nik", current, 2.0 * identity[None, :, :] - product, precision=precise_mode)

    return lax.fori_loop(0, ITERS, advance, initial)


def block_rank(block_owner):
    block_total = block_owner.shape[0]
    same_owner = block_owner[:, None] == block_owner[None, :]
    positions = jnp.arange(block_total, dtype=jnp.int32)
    before = positions[None, :] < positions[:, None]
    return jnp.sum((same_owner & before).astype(jnp.int32), axis=1)


def reference(activations, cotangent, sampled_rows, block_owner):
    grad = jnp.dot(activations.T, cotangent, preferred_element_type=jnp.float32)
    shard_base = (jnp.arange(SAMPLES, dtype=jnp.int32) // S_DEV) * TOK_DEV
    global_rows = (shard_base + sampled_rows).astype(jnp.int32)
    picked_acts = jnp.take(activations, global_rows, axis=0).astype(jnp.float32)
    picked_grads = jnp.take(cotangent, global_rows, axis=0).astype(jnp.float32)
    act_blocks = picked_acts.reshape(SAMPLES, NBLK, FACTOR_BLOCK)
    a_gram = jnp.einsum("snk,snl->nkl", act_blocks, act_blocks, precision=precise_mode)
    a_factor = a_gram / SAMPLES + DAMPING * jnp.eye(FACTOR_BLOCK, dtype=jnp.float32)[None, :, :]
    grad_groups = picked_grads.reshape(SAMPLES, N_TENSOR, GW)
    g_gram = jnp.einsum("snk,snl->nkl", grad_groups, grad_groups, precision=precise_mode)
    g_factor = g_gram * (TOKENS / SAMPLES) + DAMPING * jnp.eye(GW, dtype=jnp.float32)[None, :, :]
    input_factor_inverse = newton_inverse(a_factor)
    g_inverse = newton_inverse(g_factor)
    grad_four = grad.reshape(NBLK, FACTOR_BLOCK, N_TENSOR, GW)
    right_done = jnp.einsum("njtk,tkl->njtl", grad_four, g_inverse, precision=precise_mode)
    natural_step = jnp.einsum("nij,njtl->nitl", input_factor_inverse, right_done, precision=precise_mode).reshape(D, KVW)
    owner_slot_index = (block_owner * CAP + block_rank(block_owner)).astype(jnp.int32)
    owner_block_inverses = jnp.zeros((SLOT_TOTAL, FACTOR_BLOCK, FACTOR_BLOCK), jnp.float32).at[owner_slot_index].set(input_factor_inverse)
    return natural_step, owner_block_inverses
```

```python
import jax
import jax.numpy as jnp
from jax import lax
from jax.experimental import pallas as pl
from jax.experimental.pallas import tpu as pltpu
from jax.sharding import PartitionSpec as P

S_DEV = 64
BLK = 256
HALF = 128
ITERS = 10
DAMPING = 0.05
MESH = pl.DeviceIdType.MESH
HI = lax.Precision.HIGHEST
F32 = jnp.float32
BF16 = jnp.bfloat16


class Sems:
    def __init__(self, send, recv):
        self.send, self.recv, self.used = send, recv, 0

    def take(self, count):
        base = self.used
        self.used += count
        return base


SEM_TOTAL = 128


def dot_hi(a, b, dims=(((1,), (0,)), ((), ()))):
    return lax.dot_general(a, b, dims, precision=HI, preferred_element_type=F32)


def gram(rows):
    return lax.dot_general(rows, rows, (((0,), (0,)), ((), ())), preferred_element_type=F32)


def eye(n):
    r = lax.broadcasted_iota(jnp.int32, (n, n), 0)
    c = lax.broadcasted_iota(jnp.int32, (n, n), 1)
    return jnp.where(r == c, 1.0, 0.0).astype(F32)


def newton_inverse(m_ref, x_ref, e_ref):
    ident = eye(BLK)
    m = m_ref[...]
    bound = jnp.max(jnp.sum(jnp.abs(m), axis=1, keepdims=True), axis=0, keepdims=True)
    inv = 1.0 / bound
    e_ref[...] = ident - m * inv
    x_ref[...] = (ident + e_ref[...]) * inv
    e = e_ref[...]
    e_ref[...] = dot_hi(e, e)

    def step(k, _):
        e = e_ref[...]
        x = x_ref[...]
        both = dot_hi(jnp.concatenate([x, e], axis=0), e)
        x_ref[...] = x + both[:BLK]
        e_ref[...] = both[BLK:]
        return 0

    lax.fori_loop(0, 4, step, 0)
    e_ref[...] = ident - dot_hi(m, x_ref[...])
    lax.fori_loop(0, 4, step, 0)
    x_ref[...] += dot_hi(x_ref[...], e_ref[...])


def kernel(
    act_hbm, cot_ref, rows_ref, owned_ref,
    step_out, slot_out,
    act, lhs, buf, pairs, rs1, acc1, rs2, acc2, rs3, fin,
    picks, pg, r1, r2, g1, g2,
    gr, gx, gh, gz, need, m_ref, x_ref, e_ref, inv,
    s1, s2, dd, t1, t2, outh,
    act_sem, send_sem, recv_sem,
):
    dp = lax.axis_index("dp")
    c = lax.rem(dp, 2)
    z = lax.rem(lax.div(dp, 2), 2)
    y = lax.rem(lax.div(dp, 4), 4)
    x = lax.div(dp, 16)
    u = (1 - c) * x + c * y
    v = (1 - c) * y + c * x
    oc = 1 - c
    oz = 1 - z

    def dev(xx, yy, zz, cc):
        return ((xx * 4 + yy) * 2 + zz) * 2 + cc

    def dev_uv(uu, vv, cc):
        return dev((1 - c) * uu + c * vv, (1 - c) * vv + c * uu, z, cc)

    def wrap(a):
        return lax.rem(a, 4)

    def peer_u(k):
        return dev_uv(wrap(u + k), v, c)

    def peer_v(k):
        return dev_uv(u, wrap(v + k), c)

    peer_z = dev(x, y, oz, c)
    peer_c = dev(x, y, z, oc)

    def pair_of(uu, vv):
        return (1 - c) * (uu * 4 + vv) + c * (vv * 4 + uu)

    sems = Sems(send_sem, recv_sem)

    def rcopy(src, dst, send_i, recv_i, to):
        return pltpu.make_async_remote_copy(
            src_ref=src, dst_ref=dst, send_sem=send_sem.at[send_i], recv_sem=recv_sem.at[recv_i],
            device_id={"dp": to}, device_id_type=MESH,
        )

    def act_copy(i, p):
        cols = pl.ds(pl.multiple_of(p * 2 * BLK, 2 * BLK), 2 * BLK)
        return pltpu.make_async_copy(act_hbm.at[:, cols], act.at[:, cols], act_sem.at[i])

    def visit(i):
        a, b = lax.div(i, 4), lax.rem(i, 4)
        g = wrap(x + wrap(a + 1))
        j = wrap(y + wrap(b + 1))
        uu = (1 - c) * g + c * j
        vv = (1 - c) * j + c * g
        return g * 4 + j, uu, vv, wrap(uu - u + 4)

    def start_load(i, _):
        act_copy(i, visit(i)[0]).start()
        return 0

    lax.fori_loop(0, 16, start_load, 0)

    barrier = pltpu.get_barrier_semaphore()
    for to in [peer_u(1), peer_u(2), peer_u(3), peer_v(1), peer_v(2), peer_v(3), peer_z, peer_c]:
        pl.semaphore_signal(barrier, inc=1, device_id={"dp": to}, device_id_type=MESH)

    lhs[0:BLK, :] = cot_ref[...].T
    tok = lax.broadcasted_iota(jnp.int32, (S_DEV, lhs.shape[1]), 1)
    onehot = (tok == rows_ref[...]).astype(F32).astype(BF16)
    lhs[BLK:, :] = onehot
    pg[...] = jnp.dot(onehot, cot_ref[...], preferred_element_type=F32).astype(BF16)
    s2[2, 0, 0, :, :] = jnp.zeros((8, BLK), F32)

    pl.semaphore_wait(barrier, 8)

    pick_b = sems.take(16)
    pair_b = sems.take(16)
    rs1_b = sems.take(16)
    rows2_b = sems.take(4)
    g1_b = sems.take(4)
    g2_b = sems.take(4)
    rs2_b = sems.take(4)
    rs3_b = sems.take(1)
    rs4_b = sems.take(1)
    gx_b = sems.take(1)
    gz_b = sems.take(2)
    need_b = sems.take(1)
    inv_b = sems.take(1)
    s1_b = sems.take(4)
    s2_b = sems.take(4)
    s3_b = sems.take(1)
    t1_b = sems.take(4)
    t2_b = sems.take(4)
    out_b = sems.take(1)

    def g1_copy(k):
        return rcopy(pg, g1.at[k], g1_b + k, g1_b + k, peer_u(k))

    for k in (2, 1, 3):
        g1_copy(k).start()

    def pick_copy(i, p, uu, vv, k):
        return rcopy(
            picks.at[:, p], r1.at[:, vv, k], pick_b + i, pick_b + vv * 4 + k, dev_uv(uu, v, c)
        )

    def pair_copy(i, p):
        return rcopy(buf.at[oc, p], pairs.at[p], pair_b + i, pair_b + p, peer_c)

    def rs1_copy(i, p, uu, vv, k):
        return rcopy(
            buf.at[c, p], rs1.at[k - 1, vv], rs1_b + i, rs1_b + vv * 4 + k, dev_uv(uu, v, c)
        )

    def body(i, _):
        @pl.when(i < 16)
        def _():
            p, uu, vv, k = visit(i)
            act_copy(i, p).wait()
            cols = pl.ds(pl.multiple_of(p * 2 * BLK, 2 * BLK), 2 * BLK)
            res = jnp.dot(lhs[...], act[:, cols], preferred_element_type=F32)
            for h in range(2):
                for zz in range(2):
                    buf[h, p, zz, :, :] = res[h * HALF:(h + 1) * HALF, zz * BLK:(zz + 1) * BLK]
            for zz in range(2):
                picks[zz, p, :, :] = res[BLK:, zz * BLK:(zz + 1) * BLK].astype(BF16)
            pair_copy(i, p).start()

            @pl.when(k != 0)
            def _():
                pick_copy(i, p, uu, vv, k).start()

            @pl.when(k == 0)
            def _():
                r1[:, vv, 0, :, :] = picks[:, p, :, :]

        @pl.when(i >= 3)
        def _():
            p, uu, vv, k = visit(i - 3)
            pair_copy(i - 3, p).wait_recv()
            buf[c, p, :, :, :] = buf[c, p, :, :, :] + pairs[p, :, :, :]

            @pl.when(k != 0)
            def _():
                rs1_copy(i - 3, p, uu, vv, k).start()

        return 0

    lax.fori_loop(0, 19, body, 0)

    for k in (2, 1, 3):
        g1_copy(k).wait_recv()
    g1[0, :, :] = pg[...]

    def g2_copy(k):
        return rcopy(g1, g2.at[k], g2_b + k, g2_b + k, peer_v(k))

    def rows2_copy(k):
        return rcopy(r1.at[:, wrap(v + k)], r2.at[:, k], rows2_b + k, rows2_b + k, peer_v(k))

    def pick_wait(vv, k):
        rcopy(picks.at[:, 0], r1.at[:, vv, k], pick_b, pick_b + vv * 4 + k, peer_u(k)).wait_recv()

    for k in (2, 1, 3):
        for kk in (1, 2, 3):
            pick_wait(wrap(v + k), kk)
        rows2_copy(k).start()
        g2_copy(k).start()
    for kk in (1, 2, 3):
        pick_wait(v, kk)

    for zz in range(2):
        got = gram(r1[zz, v, :, :, :].reshape(4 * S_DEV, BLK))
        gr[zz, 0, :, :] = got[:HALF]
        gr[zz, 1, :, :] = got[HALF:]
    got = gram(g1[...].reshape(4 * S_DEV, BLK))
    gr[2, 0, :, :] = got[:HALF]
    gr[2, 1, :, :] = got[HALF:]
    for k in (1, 3, 2):
        rows2_copy(k).wait_recv()
        g2_copy(k).wait_recv()
        for zz in range(3):
            if zz < 2:
                got = gram(r2[zz, k, :, :, :].reshape(4 * S_DEV, BLK))
            else:
                got = gram(g2[k, :, :, :].reshape(4 * S_DEV, BLK))
            gr[zz, 0, :, :] += got[:HALF]
            gr[zz, 1, :, :] += got[HALF:]
    gx_copy = rcopy(gr.at[:, oc], gx, gx_b, gx_b, peer_c)
    gx_copy.start()
    gx_copy.wait_recv()
    gh[...] = gr[:, c, :, :] + gx[...]
    gz_copies = [
        rcopy(gh.at[oz], gz.at[0], gz_b, gz_b, peer_z),
        rcopy(gh.at[2], gz.at[1], gz_b + 1, gz_b + 1, peer_z),
    ]
    for copy in gz_copies:
        copy.start()
    for copy in gz_copies:
        copy.wait_recv()
    need[0, c, :, :] = gh[z, :, :] + gz[0, :, :]
    need[1, c, :, :] = gh[2, :, :] + gz[1, :, :]
    need_copy = rcopy(need.at[oc, c], need.at[oc, c], need_b, need_b, peer_c)
    need_copy.start()
    need_copy.wait_recv()
    cf = c.astype(F32)
    scale = (1.0 - cf) / 4096.0 + cf * 12.0
    m_ref[...] = need[c, :, :, :].reshape(BLK, BLK) * scale + DAMPING * eye(BLK)
    newton_inverse(m_ref, x_ref, e_ref)
    inv[c, :, :, :, :, :] = x_ref[...].reshape(2, 4, 4, 8, BLK)
    inv_copy = rcopy(inv.at[c], inv.at[c], inv_b, inv_b, peer_c)
    inv_copy.start()

    def rs1_wait(vv, k):
        rcopy(
            buf.at[c, 0], rs1.at[k - 1, vv], rs1_b, rs1_b + vv * 4 + k, peer_u(k)
        ).wait_recv()

    def rs2_copy(k):
        return rcopy(
            acc1.at[wrap(v + k)], rs2.at[k], rs2_b + k, rs2_b + k, peer_v(k)
        )

    for k in (2, 1, 3, 0):
        vv = wrap(v + k)
        for kk in (1, 2, 3):
            rs1_wait(vv, kk)
        acc1[vv, :, :, :] = (
            buf[c, pair_of(u, vv), :, :, :] + rs1[0, vv, :, :, :]
            + rs1[1, vv, :, :, :] + rs1[2, vv, :, :, :]
        )
        if k:
            rs2_copy(k).start()

    inv_copy.wait_recv()

    def s1_copy(k):
        return rcopy(inv.at[0, c, wrap(u + k)], s1.at[k], s1_b + k, s1_b + k, peer_u(k))

    for k in (2, 1, 3):
        s1_copy(k).start()
    s1[0, :, :, :] = inv[0, c, u, :, :, :]
    for k in (1, 3, 2):
        s1_copy(k).wait_recv()

    def s2_copy(k):
        return rcopy(
            s1.at[:, wrap(v + k)], s2.at[0, k], s2_b + k, s2_b + k, peer_v(k)
        )

    for k in (2, 1, 3):
        s2_copy(k).start()
    s2[0, 0, :, :, :] = s1[:, v, :, :]
    for k in (1, 3, 2):
        s2_copy(k).wait_recv()
    s3_copy = rcopy(s2.at[0], s2.at[1], s3_b, s3_b, peer_z)
    s3_copy.start()

    for k in (1, 3, 2):
        rs2_copy(k).wait_recv()
    acc2[...] = acc1[v, :, :, :] + rs2[1, :, :, :] + rs2[2, :, :, :] + rs2[3, :, :, :]
    rs3_copy = rcopy(acc2.at[oz], rs3, rs3_b, rs3_b, peer_z)
    rs3_copy.start()

    s3_copy.wait_recv()
    for kv in range(4):
        for ku in range(4):
            for cc in range(2):
                b = owned_ref[dev_uv(wrap(u + ku), wrap(v + kv), cc)]
                bb = jnp.maximum(b, 0)
                bz = lax.rem(bb, 2)
                by = lax.rem(lax.div(bb, 2), 4)
                bx = lax.div(bb, 8)
                bu = (1 - c) * bx + c * by
                bv = (1 - c) * by + c * bx
                hop = wrap(bz - z + 4)
                zi = lax.rem(hop, 2)
                none = b < 0
                i0 = jnp.where(none, 2, zi)
                i1 = jnp.where(none, 0, wrap(v - bv + 4))
                i2 = jnp.where(none, 0, wrap(u - bu + 4))
                dd[kv, ku, cc, :, :] = s2[i0, i1, i2, :, :]

    def t1_copy(k):
        return rcopy(dd.at[k], t1.at[k], t1_b + k, t1_b + k, peer_v(k))

    for k in (2, 1, 3):
        t1_copy(k).start()
    t1[0, :, :, :, :] = dd[0, :, :, :, :]

    rs3_copy.wait_recv()
    fin[c, :, :] = acc2[z, :, :] + rs3[...]
    rs4_copy = rcopy(fin.at[c], fin.at[c], rs4_b, rs4_b, peer_c)
    rs4_copy.start()

    for k in (1, 3, 2):
        t1_copy(k).wait_recv()

    def t2_copy(k):
        return rcopy(t1.at[:, k], t2.at[k], t2_b + k, t2_b + k, peer_u(k))

    for k in (2, 1, 3):
        t2_copy(k).start()
    t2[0, :, :, :, :] = t1[:, 0, :, :, :]

    rs4_copy.wait_recv()
    left = dot_hi(
        inv[0, c, :, :, :, :].reshape(HALF, BLK), fin[...].reshape(BLK, BLK), (((1,), (1,)), ((), ()))
    )
    step_out[...] = dot_hi(left, inv[1, :, :, :, :, :].reshape(BLK, BLK))

    for k in (1, 3, 2):
        t2_copy(k).wait_recv()
    for ku in range(4):
        for kv in range(4):
            row = wrap(u - ku + 4) * 4 + wrap(v - kv + 4)
            for cc in range(2):
                outh[cc, 0, row, :, :] = t2[ku, kv, cc, :, :]
    out_copy = rcopy(outh.at[oc, 0], outh.at[oc, 1], out_b, out_b, peer_c)
    out_copy.start()
    out_copy.wait_recv()
    slot_out[0, pl.ds(pl.multiple_of(c * HALF, HALF), HALF), :] = outh[c, 0, :, :, :].reshape(HALF, BLK)
    slot_out[0, pl.ds(pl.multiple_of(oc * HALF, HALF), HALF), :] = outh[c, 1, :, :, :].reshape(HALF, BLK)

    def drain(i, _):
        p, uu, vv, k = visit(i)
        pair_copy(i, p).wait_send()

        @pl.when(k != 0)
        def _():
            pick_copy(i, p, uu, vv, k).wait_send()
            rs1_copy(i, p, uu, vv, k).wait_send()

        return 0

    lax.fori_loop(0, 16, drain, 0)
    for k in (1, 2, 3):
        for make in (g1_copy, g2_copy, rows2_copy, rs2_copy, s1_copy, s2_copy, t1_copy, t2_copy):
            make(k).wait_send()
    for copy in [gx_copy, *gz_copies, need_copy, inv_copy, s3_copy, rs3_copy, rs4_copy, out_copy]:
        copy.wait_send()


def per_device(activations, cotangent, sampled_rows, block_owner):
    tokens, width = activations.shape
    ids = jnp.arange(64, dtype=jnp.int32)
    blocks = jnp.arange(block_owner.shape[0], dtype=jnp.int32)
    owned = jnp.max(
        jnp.where(block_owner[None, :] == ids[:, None], blocks[None, :], -1), axis=1
    )
    vmem = pltpu.VMEM
    return pl.pallas_call(
        kernel,
        out_shape=(
            jax.ShapeDtypeStruct((HALF, BLK), F32),
            jax.ShapeDtypeStruct((1, BLK, BLK), F32),
        ),
        in_specs=[
            pl.BlockSpec(memory_space=pl.ANY),
            pl.BlockSpec(memory_space=pltpu.VMEM),
            pl.BlockSpec(memory_space=pltpu.VMEM),
            pl.BlockSpec(memory_space=pltpu.SMEM),
        ],
        out_specs=(
            pl.BlockSpec(memory_space=pltpu.VMEM),
            pl.BlockSpec(memory_space=pltpu.VMEM),
        ),
        scratch_shapes=[
            vmem((tokens, width), BF16),
            vmem((BLK + S_DEV, tokens), BF16),
            vmem((2, 16, 2, HALF, BLK), F32),
            vmem((16, 2, HALF, BLK), F32),
            vmem((3, 4, 2, HALF, BLK), F32),
            vmem((4, 2, HALF, BLK), F32),
            vmem((4, 2, HALF, BLK), F32),
            vmem((2, HALF, BLK), F32),
            vmem((HALF, BLK), F32),
            vmem((2, HALF, BLK), F32),
            vmem((2, 16, S_DEV, BLK), BF16),
            vmem((S_DEV, BLK), BF16),
            vmem((2, 4, 4, S_DEV, BLK), BF16),
            vmem((2, 4, 4, S_DEV, BLK), BF16),
            vmem((4, S_DEV, BLK), BF16),
            vmem((4, 4, S_DEV, BLK), BF16),
            vmem((3, 2, HALF, BLK), F32),
            vmem((3, HALF, BLK), F32),
            vmem((3, HALF, BLK), F32),
            vmem((2, HALF, BLK), F32),
            vmem((2, 2, HALF, BLK), F32),
            vmem((BLK, BLK), F32),
            vmem((BLK, BLK), F32),
            vmem((BLK, BLK), F32),
            vmem((2, 2, 4, 4, 8, BLK), F32),
            vmem((4, 4, 8, BLK), F32),
            vmem((3, 4, 4, 8, BLK), F32),
            vmem((4, 4, 2, 8, BLK), F32),
            vmem((4, 4, 2, 8, BLK), F32),
            vmem((4, 4, 2, 8, BLK), F32),
            vmem((2, 2, 16, 8, BLK), F32),
            pltpu.SemaphoreType.DMA((16,)),
            pltpu.SemaphoreType.DMA((SEM_TOTAL,)),
            pltpu.SemaphoreType.DMA((SEM_TOTAL,)),
        ],
        compiler_params=pltpu.CompilerParams(
            collective_id=0, has_side_effects=True, vmem_limit_bytes=60 * 1024 * 1024
        ),
    )(activations, cotangent, sampled_rows.reshape(S_DEV, 1), owned)


def solution(mesh):
    return jax.shard_map(
        per_device,
        mesh=mesh,
        in_specs=(P("dp", None), P("dp", "tensor"), P("dp"), P()),
        out_specs=(P("dp", "tensor"), P("dp", None, None)),
        check_vma=False,
    )
```

```python
import jax
import jax.numpy as jnp
from jax import lax
from jax.experimental import pallas as pl
from jax.experimental.pallas import tpu as pltpu
from jax.sharding import PartitionSpec as P

S_DEV = 64
BLK = 256
HALF = 128
ITERS = 10
DAMPING = 0.05
MESH = pl.DeviceIdType.MESH
HI = lax.Precision.HIGHEST
F32 = jnp.float32
BF16 = jnp.bfloat16


class Sems:
    def __init__(self):
        self.used = 0

    def take(self, count):
        base = self.used
        self.used += count
        return base


SEM_TOTAL = 144
LAG = 3
REL_EARLY = 2
GRAD_ORDER = (
    (2, 2), (2, 1), (1, 2), (2, 3), (3, 2), (2, 0), (0, 2),
    (1, 1), (1, 3), (3, 1), (3, 3), (1, 0), (0, 1), (3, 0), (0, 3), (0, 0),
)


def dot_hi(a, b, dims=(((1,), (0,)), ((), ()))):
    return lax.dot_general(a, b, dims, precision=HI, preferred_element_type=F32)


def gram(rows):
    return lax.dot_general(rows, rows, (((0,), (0,)), ((), ())), preferred_element_type=F32)


def eye(n):
    r = lax.broadcasted_iota(jnp.int32, (n, n), 0)
    c = lax.broadcasted_iota(jnp.int32, (n, n), 1)
    return jnp.where(r == c, 1.0, 0.0).astype(F32)


def newton_step(x_ref, e_ref):
    def step(k, _):
        e = e_ref[...]
        x = x_ref[...]
        both = dot_hi(jnp.concatenate([x, e], axis=0), e)
        x_ref[...] = x + both[:BLK]
        e_ref[...] = both[BLK:]
        return 0

    return step


def newton_begin(m_ref, x_ref, e_ref):
    ident = eye(BLK)
    m = m_ref[...]
    bound = jnp.max(jnp.sum(jnp.abs(m), axis=1, keepdims=True), axis=0, keepdims=True)
    inv = 1.0 / bound
    e = ident - m * inv
    x_ref[...] = (ident + e) * inv
    e_ref[...] = dot_hi(e, e)
    lax.fori_loop(0, 4, newton_step(x_ref, e_ref), 0)
    e_ref[...] = ident - dot_hi(m, x_ref[...])


def newton_end(x_ref, e_ref):
    lax.fori_loop(0, 4, newton_step(x_ref, e_ref), 0)
    x_ref[...] += dot_hi(x_ref[...], e_ref[...])


def kernel(
    act_hbm, cot_hbm, rows_ref, owner_ref,
    step_hbm, slot_hbm,
    act, cot_ref, cott, onehot, buf, pairs, rel, rs1, acc1, rs2, acc2, rs3, fin,
    picks, pg, r1, r2, g1, g2,
    gr, gx, gh, gz, m_ref, x_ref, e_ref, isl, isx, ginv,
    ss, dd, tt, outh, slot_v, step_v, table,
    act_sem, out_sem, send_sem, recv_sem,
):
    dp = lax.axis_index("dp")
    ten = lax.axis_index("tensor")
    c = lax.rem(dp, 2)
    z = lax.rem(lax.div(dp, 2), 2)
    y = lax.rem(lax.div(dp, 4), 4)
    x = lax.div(dp, 16)
    u = (1 - c) * x + c * y
    v = (1 - c) * y + c * x
    oc = 1 - c
    oz = 1 - z

    def wrap(a):
        return lax.rem(a, 4)

    def dev(xx, yy, zz, cc):
        return ((xx * 4 + yy) * 2 + zz) * 2 + cc

    def dev_uv(uu, vv, cc):
        return dev((1 - c) * uu + c * vv, (1 - c) * vv + c * uu, z, cc)

    def at(d):
        return {"dp": d, "tensor": ten}

    def peer_u(k):
        return at(dev_uv(wrap(u + k), v, c))

    def peer_v(k):
        return at(dev_uv(u, wrap(v + k), c))

    peer_z = at(dev(x, y, oz, c))
    peer_w = {"dp": dev(x, y, oz, c), "tensor": wrap(ten + 3 + 2 * z)}
    peer_c = at(dev(x, y, z, oc))

    def pair_of(uu, vv):
        return (1 - c) * (uu * 4 + vv) + c * (vv * 4 + uu)

    sems = Sems()

    def rcopy(src, dst, send_i, recv_i, to):
        return pltpu.make_async_remote_copy(
            src_ref=src, dst_ref=dst, send_sem=send_sem.at[send_i], recv_sem=recv_sem.at[recv_i],
            device_id=to, device_id_type=MESH,
        )

    def columns(p):
        return pl.ds(pl.multiple_of(p * 2 * BLK, 2 * BLK), 2 * BLK)

    def act_copy(i, p):
        return pltpu.make_async_copy(act_hbm.at[:, columns(p)], act.at[:, columns(p)], act_sem.at[i])

    def visit(i):
        g = wrap(x + wrap(lax.div(i, 4) + 1))
        j = wrap(y + wrap(lax.rem(i, 4) + 1))
        uu = (1 - c) * g + c * j
        vv = (1 - c) * j + c * g
        return g * 4 + j, uu, vv, wrap(uu - u + 4)

    def start_load(i, _):
        act_copy(i, visit(i)[0]).start()
        return 0

    lax.fori_loop(0, 16, start_load, 0)
    cot_copy = pltpu.make_async_copy(cot_hbm, cot_ref, act_sem.at[16])
    cot_copy.start()

    barrier = pltpu.get_barrier_semaphore()

    def chip(n):
        dz, dx, dy = lax.div(n, 16), lax.rem(lax.div(n, 4), 4), lax.rem(n, 4)
        xx, yy, zz = wrap(x + dx), wrap(y + dy), lax.rem(z + dz, 2)
        return xx, yy, zz, dz, dx, dy

    def chip_dev(n):
        xx, yy, zz, dz, dx, dy = chip(n)
        other = dz * lax.rem(dx + dy, 2)
        return {"dp": dev(xx, yy, zz, c), "tensor": wrap(ten + other * (3 + 2 * z))}

    def greet(n, _):
        pl.semaphore_signal(barrier, inc=1, device_id=chip_dev(n), device_id_type=MESH)
        return 0

    lax.fori_loop(1, 32, greet, 0)
    for to in [peer_w, peer_c]:
        pl.semaphore_signal(barrier, inc=1, device_id=to, device_id_type=MESH)

    r_i = lax.broadcasted_iota(jnp.int32, (S_DEV, S_DEV), 0)
    c_i = lax.broadcasted_iota(jnp.int32, (S_DEV, S_DEV), 1)
    rows = jnp.broadcast_to(rows_ref[...].astype(F32), (S_DEV, S_DEV))
    row_col = jnp.sum(jnp.where(r_i == c_i, rows, 0.0), axis=1, keepdims=True)
    tok = lax.broadcasted_iota(jnp.int32, onehot.shape, 1).astype(F32)
    onehot[...] = jnp.where(tok == row_col, 1.0, 0.0).astype(BF16)
    ss[2, 0, 0, :, :] = jnp.zeros((8, HALF), F32)

    pick_b = sems.take(16)
    pair_b = sems.take(16)
    rel_b = sems.take(4)
    rsp_b = sems.take(8)
    rows2_b = sems.take(4)
    g1_b = sems.take(4)
    g2_b = sems.take(4)
    rs2_b = sems.take(4)
    rs3_b = sems.take(1)
    rs4_b = sems.take(1)
    gx_b = sems.take(3)
    gz_b = sems.take(3)
    inv_b = sems.take(2)
    s_b = sems.take(32)
    t_b = sems.take(32)
    out_b = sems.take(1)

    def pick_copy(i, p, uu, vv, k):
        return rcopy(
            picks.at[:, p], r1.at[:, vv, k], pick_b + i, pick_b + vv * 4 + k, at(dev_uv(uu, v, c))
        )

    def pick_body(i, _):
        p = visit(i)[0]
        act_copy(i, p).wait()
        res = jnp.dot(onehot[...], act[:, columns(p)], preferred_element_type=F32).astype(BF16)
        for zz in range(2):
            picks[zz, p, :, :] = res[:, zz * BLK:(zz + 1) * BLK]
        return 0

    def pick_send(i, _):
        p, uu, vv, k = visit(i)

        @pl.when(k != 0)
        def _():
            pick_copy(i, p, uu, vv, k).start()

        @pl.when(k == 0)
        def _():
            r1[:, vv, 0, :, :] = picks[:, p, :, :]

        return 0

    with jax.named_scope("picks"):
        lax.fori_loop(0, 16, pick_body, 0)
    cot_copy.wait()
    pg[...] = jnp.dot(onehot[...], cot_ref[...], preferred_element_type=F32).astype(BF16)

    def g1_copy(k):
        return rcopy(pg, g1.at[k], g1_b + k, g1_b + k, peer_u(k))

    with jax.named_scope("barrier"):
        pl.semaphore_wait(barrier, 33)
    lax.fori_loop(0, 16, pick_send, 0)
    for k in (2, 1, 3):
        g1_copy(k).start()
    cott[...] = cot_ref[...].T

    def grad_pair(i):
        code = jnp.int32(0)
        for n, (a, b) in enumerate(GRAD_ORDER):
            code = jnp.where(i == n, a * 4 + b, code)
        return wrap(x + lax.div(code, 4)) * 4 + wrap(y + lax.rem(code, 4))

    def pair_copy(i, p):
        return rcopy(buf.at[oc, p], pairs.at[p], pair_b + i, pair_b + p, peer_c)

    def grad_part(i):
        p = grad_pair(i)
        res = jnp.dot(cott[...], act[:, columns(p)], preferred_element_type=F32)
        for h in range(2):
            for zz in range(2):
                buf[h, p, zz, :, :] = res[h * HALF:(h + 1) * HALF, zz * BLK:(zz + 1) * BLK]
        pair_copy(i, p).start()

    def pair_sum(i):
        p = grad_pair(i)
        pair_copy(i, p).wait_recv()
        buf[c, p, :, :, :] = buf[c, p, :, :, :] + pairs[p, :, :, :]

    def early(i, _):
        grad_part(i)
        return 0

    def late(i, _):
        grad_part(i)
        pair_sum(i - LAG)
        return 0

    def rest(i, _):
        pair_sum(i)
        return 0

    UP, DOWN = (2, 1), (3, 0)

    def block(k, m):
        return buf.at[c, pair_of(wrap(u + k), wrap(v + m))]

    def rel_copy(k, n):
        m = (UP if k == 1 else DOWN)[n]
        i = rel_b + (k // 2) * 2 + n
        return rcopy(block(2, m), rel.at[k // 2, n], i, i, peer_u(k))

    def rs1_copy(k, m):
        i = rsp_b + (k // 2) * 4 + m
        return rcopy(block(k, m), rs1.at[k // 2, m], i, i, peer_u(k))

    with jax.named_scope("grad_a"):
        lax.fori_loop(0, LAG, early, 0)
        lax.fori_loop(LAG, 7 + LAG, late, 0)
    for n in range(REL_EARLY):
        for k in (1, 3):
            rel_copy(k, n).start()
    with jax.named_scope("grad_b"):
        lax.fori_loop(7 + LAG, 16, late, 0)

    def g2_copy(k):
        return rcopy(g1, g2.at[k], g2_b + k, g2_b + k, peer_v(k))

    def rows2_copy(k):
        return rcopy(r1.at[:, wrap(v + k)], r2.at[:, k], rows2_b + k, rows2_b + k, peer_v(k))

    def pick_wait(vv, k):
        rcopy(picks.at[:, 0], r1.at[:, vv, k], pick_b, pick_b + vv * 4 + k, peer_u(k)).wait_recv()

    with jax.named_scope("rows1wait"):
        for k in (2, 1, 3):
            for kk in (1, 2, 3):
                pick_wait(wrap(v + k), kk)
            rows2_copy(k).start()
        for k in (2, 1, 3):
            g1_copy(k).wait_recv()
        g1[0, :, :] = pg[...]
        for k in (2, 1, 3):
            g2_copy(k).start()
        for kk in (1, 2, 3):
            pick_wait(v, kk)

    with jax.named_scope("grad_c"):
        lax.fori_loop(16 - LAG, 16, rest, 0)
    for n in range(REL_EARLY, 2):
        for k in (1, 3):
            rel_copy(k, n).start()

    def fill_table(i, _):
        b = jnp.int32(-1)
        for q in range(32):
            b = jnp.where(owner_ref[q] == i, q, b)
        table[i] = b
        return 0

    with jax.named_scope("table"):
        lax.fori_loop(0, 64, fill_table, 0)

    def gx_copy(n):
        return rcopy(gr.at[n], gx.at[n], gx_b + n, gx_b + n, peer_c)

    with jax.named_scope("rows2wait"):
        for zz in range(2):
            gr[zz, :, :] = gram(r1[zz, v, :, :, :].reshape(4 * S_DEV, BLK))
        gr[2, :, :] = gram(g1[...].reshape(4 * S_DEV, BLK))
        for k in (1, 3, 2):
            rows2_copy(k).wait_recv()
            for zz in range(2):
                gr[zz, :, :] += gram(r2[zz, k, :, :, :].reshape(4 * S_DEV, BLK))

    @pl.when(c == 1)
    def _():
        gx_copy(oz).start()
        gx_copy(z).start()

    for n in range(2):
        rs1_copy(1, DOWN[n]).start()
        rs1_copy(3, UP[n]).start()

    def gz_copy(n):
        half = pl.ds(n * HALF, HALF)
        return rcopy(gh.at[half], gz.at[half], gz_b + n, gz_b + n, peer_w if n else peer_z)

    gz_all = rcopy(gh, gz, gz_b + 2, gz_b + 2, peer_z)

    @pl.when(c == 0)
    def _():
        with jax.named_scope("gx"):
            gx_copy(oz).wait_recv()
        gh[...] = gr[oz, :, :] + gx[oz, :, :]
        gz_copy(0).start()
        gz_copy(1).start()
        gx_copy(z).wait_recv()
        m_ref[...] = gr[z, :, :] + gx[z, :, :]

    with jax.named_scope("g2wait"):
        for k in (1, 3, 2):
            g2_copy(k).wait_recv()
            gr[2, :, :] += gram(g2[k, :, :, :].reshape(4 * S_DEV, BLK))

    @pl.when(c == 0)
    def _():
        gx_copy(2).start()

    @pl.when(c == 1)
    def _():
        with jax.named_scope("gxg"):
            gx_copy(2).wait_recv()
        gh[...] = gr[2, :, :] + gx[2, :, :]
        gz_all.start()
        m_ref[...] = gh[...]

    with jax.named_scope("relay"):
        for n in range(2):
            for k in (1, 3):
                rel_copy(k, n).wait_recv()
                m = (UP if k == 1 else DOWN)[n]
                p = pair_of(wrap(u + k), wrap(v + m))
                buf[c, p, :, :, :] = buf[c, p, :, :, :] + rel[k // 2, n, :, :, :]
                rs1_copy(k, m).start()

    with jax.named_scope("gz"):
        @pl.when(c == 0)
        def _():
            gz_copy(0).wait_recv()
            gz_copy(1).wait_recv()

        @pl.when(c == 1)
        def _():
            gz_all.wait_recv()

    cf = c.astype(F32)
    scale = (1.0 - cf) / 4096.0 + cf * 12.0
    m_ref[...] = (m_ref[...] + gz[...]) * scale + DAMPING * eye(BLK)
    with jax.named_scope("newton_begin"):
        newton_begin(m_ref, x_ref, e_ref)

    def s_copy(n):
        xx, yy, zz, dz, dx, dy = chip(n)
        return rcopy(isl.at[zz, xx * 4 + yy], ss.at[dz, dx, dy], s_b + n, s_b + n, chip_dev(n))

    def s_start(n, _):
        s_copy(n).start()
        return 0

    half_copy = rcopy(isx, isl, inv_b, inv_b, peer_c)
    ginv_copy = rcopy(x_ref, ginv, inv_b + 1, inv_b + 1, peer_c)

    @pl.when(c == 0)
    def _():
        with jax.named_scope("newton_end"):
            newton_end(x_ref, e_ref)
        for zz in range(2):
            cols = pl.ds(zz * HALF, HALF)
            isx[zz, :, :, :] = x_ref[HALF:, cols].reshape(16, 8, HALF)
            isl[zz, :, :, :] = x_ref[:HALF, cols].reshape(16, 8, HALF)
        half_copy.start()
        lax.fori_loop(1, 32, s_start, 0)

    @pl.when(c == 1)
    def _():
        with jax.named_scope("half"):
            half_copy.wait_recv()
        lax.fori_loop(1, 32, s_start, 0)
        with jax.named_scope("newton_end"):
            newton_end(x_ref, e_ref)
        ginv_copy.start()

    ss[0, 0, 0, :, :] = isl[z, x * 4 + y, :, :]

    def rs2_copy(k):
        return rcopy(acc1.at[k], rs2.at[k], rs2_b + k, rs2_b + k, peer_v(k))

    with jax.named_scope("rs1"):
        for m in (3, 2, 1, 0):
            rs1_copy(1, m).wait_recv()
            rs1_copy(3, m).wait_recv()
            acc1[m, :, :, :] = block(0, m)[...] + rs1[0, m, :, :, :] + rs1[1, m, :, :, :]
            if m:
                rs2_copy(m).start()

    def s_wait(n, _):
        s_copy(n).wait_recv()
        return 0

    def t_copy(n):
        xx, yy, zz, dz, dx, dy = chip(n)
        return rcopy(dd.at[dz, dx, dy], tt.at[dz, dx, dy], t_b + n, t_b + n, chip_dev(n))

    def select(n, _):
        xx, yy, zz, dz, dx, dy = chip(n)
        for cc in range(2):
            b = table[dev(xx, yy, zz, cc)]
            bb = jnp.maximum(b, 0)
            bz = lax.rem(bb, 2)
            by = lax.rem(lax.div(bb, 2), 4)
            bx = lax.div(bb, 8)
            none = b < 0
            i0 = jnp.where(none, 2, lax.rem(bz + z, 2))
            i1 = jnp.where(none, 0, wrap(x - bx + 4))
            i2 = jnp.where(none, 0, wrap(y - by + 4))
            dd[dz, dx, dy, cc, :, :] = ss[i0, i1, i2, :, :]

        @pl.when(n > 0)
        def _():
            t_copy(n).start()

        return 0

    with jax.named_scope("s"):
        lax.fori_loop(1, 32, s_wait, 0)
    with jax.named_scope("select"):
        lax.fori_loop(0, 32, select, 0)
    tt[0, 0, 0, :, :, :] = dd[0, 0, 0, :, :, :]

    with jax.named_scope("rs2"):
        for k in (3, 2, 1):
            rs2_copy(k).wait_recv()
    acc2[...] = acc1[0, :, :, :] + rs2[1, :, :, :] + rs2[2, :, :, :] + rs2[3, :, :, :]
    rs3_copy = rcopy(acc2.at[oz], rs3, rs3_b, rs3_b, peer_z)
    rs3_copy.start()

    with jax.named_scope("rs3"):
        rs3_copy.wait_recv()
    fin[c, :, :] = acc2[z, :, :] + rs3[...]
    rs4_copy = rcopy(fin.at[c], fin.at[c], rs4_b, rs4_b, peer_c)
    rs4_copy.start()

    def t_wait(n, _):
        t_copy(n).wait_recv()
        return 0

    def assemble(n, _):
        dz, dx, dy = lax.div(n, 16), lax.rem(lax.div(n, 4), 4), lax.rem(n, 4)
        row = wrap(x - dx + 4) * 4 + wrap(y - dy + 4)
        zz = lax.rem(z + dz, 2)
        for cc in range(2):
            outh[cc, 0, zz, row, :, :] = tt[dz, dx, dy, cc, :, :]
        return 0

    with jax.named_scope("t"):
        lax.fori_loop(1, 32, t_wait, 0)
    lax.fori_loop(0, 32, assemble, 0)
    out_copy = rcopy(outh.at[oc, 0], outh.at[oc, 1], out_b, out_b, peer_c)
    out_copy.start()

    with jax.named_scope("rs4"):
        rs4_copy.wait_recv()

    @pl.when(c == 0)
    def _():
        ginv_copy.wait_recv()

    @pl.when(c == 1)
    def _():
        ginv[...] = x_ref[...]

    with jax.named_scope("final"):
        grad = fin[...].reshape(BLK, BLK)
        nt = (((1,), (1,)), ((), ()))
        left = dot_hi(isl[0, :, :, :].reshape(HALF, HALF), grad[:, :HALF], nt)
        left += dot_hi(isl[1, :, :, :].reshape(HALF, HALF), grad[:, HALF:], nt)
        step_v[...] = dot_hi(left, ginv[...])
    step_copy = pltpu.make_async_copy(step_v, step_hbm, out_sem.at[0])
    step_copy.start()

    with jax.named_scope("outx"):
        out_copy.wait_recv()
    for n in range(2):
        h = (1 - n) * c + n * oc
        for zz in range(2):
            slot_v[h, :, zz * HALF:(zz + 1) * HALF] = outh[c, n, zz, :, :, :].reshape(HALF, HALF)
    slot_copy = pltpu.make_async_copy(slot_v, slot_hbm, out_sem.at[1])
    slot_copy.start()

    def drain(i, _):
        pair_copy(i, grad_pair(i)).wait_send()
        p, uu, vv, k = visit(i)

        @pl.when(k != 0)
        def _():
            pick_copy(i, p, uu, vv, k).wait_send()

        return 0

    def drain_slots(n, _):
        s_copy(n).wait_send()
        t_copy(n).wait_send()
        return 0

    with jax.named_scope("drain"):
        lax.fori_loop(0, 16, drain, 0)
        lax.fori_loop(1, 32, drain_slots, 0)

        @pl.when(c == 0)
        def _():
            for copy in [gx_copy(2), gz_copy(0), gz_copy(1), half_copy]:
                copy.wait_send()

        @pl.when(c == 1)
        def _():
            for copy in [gx_copy(oz), gx_copy(z), gz_all, ginv_copy]:
                copy.wait_send()

        for n in range(2):
            for k in (1, 3):
                rel_copy(k, n).wait_send()
        for m in range(4):
            for k in (1, 3):
                rs1_copy(k, m).wait_send()
        for k in (1, 2, 3):
            for make in (g1_copy, g2_copy, rows2_copy, rs2_copy):
                make(k).wait_send()
        for copy in [rs3_copy, rs4_copy, out_copy]:
            copy.wait_send()
    with jax.named_scope("store"):
        step_copy.wait()
        slot_copy.wait()


def per_device(activations, cotangent, sampled_rows, block_owner):
    tokens, width = activations.shape
    vmem = pltpu.VMEM
    step, slot = pl.pallas_call(
        kernel,
        out_shape=(
            jax.ShapeDtypeStruct((HALF, BLK), F32),
            jax.ShapeDtypeStruct((2, HALF, BLK), F32),
        ),
        in_specs=[
            pl.BlockSpec(memory_space=pl.ANY),
            pl.BlockSpec(memory_space=pl.ANY),
            pl.BlockSpec(memory_space=pltpu.VMEM),
            pl.BlockSpec(memory_space=pltpu.SMEM),
        ],
        out_specs=(
            pl.BlockSpec(memory_space=pl.ANY),
            pl.BlockSpec(memory_space=pl.ANY),
        ),
        scratch_shapes=[
            vmem((tokens, width), BF16),
            vmem((tokens, BLK), BF16),
            vmem((BLK, tokens), BF16),
            vmem((S_DEV, tokens), BF16),
            vmem((2, 16, 2, HALF, BLK), F32),
            vmem((16, 2, HALF, BLK), F32),
            vmem((2, 2, 2, HALF, BLK), F32),
            vmem((2, 4, 2, HALF, BLK), F32),
            vmem((4, 2, HALF, BLK), F32),
            vmem((4, 2, HALF, BLK), F32),
            vmem((2, HALF, BLK), F32),
            vmem((HALF, BLK), F32),
            vmem((2, HALF, BLK), F32),
            vmem((2, 16, S_DEV, BLK), BF16),
            vmem((S_DEV, BLK), BF16),
            vmem((2, 4, 4, S_DEV, BLK), BF16),
            vmem((2, 4, 4, S_DEV, BLK), BF16),
            vmem((4, S_DEV, BLK), BF16),
            vmem((4, 4, S_DEV, BLK), BF16),
            vmem((3, BLK, BLK), F32),
            vmem((3, BLK, BLK), F32),
            vmem((BLK, BLK), F32),
            vmem((BLK, BLK), F32),
            vmem((BLK, BLK), F32),
            vmem((BLK, BLK), F32),
            vmem((BLK, BLK), F32),
            vmem((2, 16, 8, HALF), F32),
            vmem((2, 16, 8, HALF), F32),
            vmem((BLK, BLK), F32),
            vmem((3, 4, 4, 8, HALF), F32),
            vmem((2, 4, 4, 2, 8, HALF), F32),
            vmem((2, 4, 4, 2, 8, HALF), F32),
            vmem((2, 2, 2, 16, 8, HALF), F32),
            vmem((2, HALF, BLK), F32),
            vmem((HALF, BLK), F32),
            pltpu.SMEM((64,), jnp.int32),
            pltpu.SemaphoreType.DMA((17,)),
            pltpu.SemaphoreType.DMA((2,)),
            pltpu.SemaphoreType.DMA((SEM_TOTAL,)),
            pltpu.SemaphoreType.DMA((SEM_TOTAL,)),
        ],
        compiler_params=pltpu.CompilerParams(
            collective_id=0, has_side_effects=True, vmem_limit_bytes=60 * 1024 * 1024
        ),
    )(activations, cotangent, sampled_rows.reshape(1, S_DEV), block_owner)
    return step, slot.reshape(1, BLK, BLK)


def solution(mesh):
    return jax.shard_map(
        per_device,
        mesh=mesh,
        in_specs=(P("dp", None), P("dp", "tensor"), P("dp"), P()),
        out_specs=(P("dp", "tensor"), P("dp", None, None)),
        check_vma=False,
    )
```

```python
import jax
import jax.numpy as jnp
from jax import lax
from jax.experimental import pallas as pl
from jax.experimental.pallas import tpu as pltpu
from jax.sharding import PartitionSpec as P

S_DEV = 64
BLK = 256
HALF = 128
ITERS = 10
DAMPING = 0.05
MESH = pl.DeviceIdType.MESH
HI = lax.Precision.HIGHEST
F32 = jnp.float32
BF16 = jnp.bfloat16


class Sems:
    def __init__(self):
        self.used = 0

    def __call__(self, count=1):
        base = self.used
        self.used += count
        return base


SENDS = 24
RECVS = 64
LAG = 3
GRAD_SPLIT = 11
PICKS_FIRST = 8
TAIL = 32
MAIN = HALF - TAIL
SENT = BLK - TAIL
GRAD_ORDER = (
    (2, 2), (2, 1), (1, 2), (2, 3), (3, 2), (2, 0), (0, 2),
    (1, 1), (1, 3), (3, 1), (3, 3), (1, 0), (0, 1), (3, 0), (0, 3), (0, 0),
)


def dot_hi(a, b, dims=(((1,), (0,)), ((), ()))):
    return lax.dot_general(a, b, dims, precision=HI, preferred_element_type=F32)


def gram(rows):
    return lax.dot_general(rows, rows, (((0,), (0,)), ((), ())), preferred_element_type=F32)


def eye(n):
    r = lax.broadcasted_iota(jnp.int32, (n, n), 0)
    c = lax.broadcasted_iota(jnp.int32, (n, n), 1)
    return jnp.where(r == c, 1.0, 0.0).astype(F32)


def newton_step(x_ref, e_ref):
    def step(k, _):
        e = e_ref[...]
        x = x_ref[...]
        both = dot_hi(jnp.concatenate([x, e], axis=0), e)
        x_ref[...] = x + both[:BLK]
        e_ref[...] = both[BLK:]
        return 0

    return step


def newton_begin(m_ref, x_ref, e_ref):
    ident = eye(BLK)
    m = m_ref[...]
    bound = jnp.max(jnp.sum(jnp.abs(m), axis=1, keepdims=True), axis=0, keepdims=True)
    inv = 1.0 / bound
    e = ident - m * inv
    x_ref[...] = (ident + e) * inv
    e_ref[...] = dot_hi(e, e)
    lax.fori_loop(0, 4, newton_step(x_ref, e_ref), 0)
    e_ref[...] = ident - dot_hi(m, x_ref[...])


def newton_end(x_ref, e_ref):
    lax.fori_loop(0, 4, newton_step(x_ref, e_ref), 0)
    x_ref[...] += dot_hi(x_ref[...], e_ref[...])


def kernel(
    act_hbm, cot_hbm, rows_ref, owner_ref,
    step_hbm, slot_hbm,
    act, cot_ref, cott, onehot, buf, pairs, zb, rel, rs1, acc1, rs2a, rs2b, acc2, rs3, fin,
    picks, pg, r1, r2, g1, g2,
    gr, gx, gh, gz, m_ref, x_ref, e_ref, isl, isx, ginv,
    ss, dd, tt, outh, slot_v, step_v, table,
    act_sem, out_sem, send_sem, recv_sem,
):
    dp = lax.axis_index("dp")
    ten = lax.axis_index("tensor")
    c = lax.rem(dp, 2)
    z = lax.rem(lax.div(dp, 2), 2)
    y = lax.rem(lax.div(dp, 4), 4)
    x = lax.div(dp, 16)
    u = (1 - c) * x + c * y
    v = (1 - c) * y + c * x
    oc = 1 - c
    oz = 1 - z

    def wrap(a):
        return lax.rem(a, 4)

    def dev(xx, yy, zz, cc):
        return ((xx * 4 + yy) * 2 + zz) * 2 + cc

    def dev_uv(uu, vv, cc):
        return dev((1 - c) * uu + c * vv, (1 - c) * vv + c * uu, z, cc)

    def at(d):
        return {"dp": d, "tensor": ten}

    def peer_u(k):
        return at(dev_uv(wrap(u + k), v, c))

    def peer_v(k):
        return at(dev_uv(u, wrap(v + k), c))

    peer_z = at(dev(x, y, oz, c))
    peer_w = {"dp": dev(x, y, oz, c), "tensor": wrap(ten + 3 + 2 * z)}
    peer_c = at(dev(x, y, z, oc))

    def pair_of(uu, vv):
        return (1 - c) * (uu * 4 + vv) + c * (vv * 4 + uu)

    sends, recvs = Sems(), Sems()

    def rcopy(src, dst, send_i, recv_i, to):
        return pltpu.make_async_remote_copy(
            src_ref=src, dst_ref=dst, send_sem=send_sem.at[send_i], recv_sem=recv_sem.at[recv_i],
            device_id=to, device_id_type=MESH,
        )

    def wait_sent(ref, send_i):
        rcopy(ref, ref, send_i, 0, peer_c).wait_send()

    def wait_got(ref, recv_i):
        rcopy(ref, ref, 0, recv_i, peer_c).wait_recv()

    def columns(p):
        return pl.ds(pl.multiple_of(p * 2 * BLK, 2 * BLK), 2 * BLK)

    def act_copy(i, p):
        return pltpu.make_async_copy(act_hbm.at[:, columns(p)], act.at[:, columns(p)], act_sem.at[i])

    def visit(i):
        g = wrap(x + wrap(lax.div(i, 4) + 1))
        j = wrap(y + wrap(lax.rem(i, 4) + 1))
        uu = (1 - c) * g + c * j
        vv = (1 - c) * j + c * g
        return g * 4 + j, uu, vv, wrap(uu - u + 4)

    def start_load(i, _):
        act_copy(i, visit(i)[0]).start()
        return 0

    barrier = pltpu.get_barrier_semaphore()

    def chip(n):
        dz, dx, dy = lax.div(n, 16), lax.rem(lax.div(n, 4), 4), lax.rem(n, 4)
        xx, yy, zz = wrap(x + dx), wrap(y + dy), lax.rem(z + dz, 2)
        return xx, yy, zz, dz, dx, dy

    def chip_dev(n):
        xx, yy, zz, dz, dx, dy = chip(n)
        other = dz * lax.rem(dx + dy, 2)
        return {"dp": dev(xx, yy, zz, c), "tensor": wrap(ten + other * (3 + 2 * z))}

    def greet(n, _):
        pl.semaphore_signal(barrier, inc=1, device_id=chip_dev(32 - n), device_id_type=MESH)
        return 0

    lax.fori_loop(1, 32, greet, 0)
    for to in [peer_w, peer_c]:
        pl.semaphore_signal(barrier, inc=1, device_id=to, device_id_type=MESH)
    lax.fori_loop(0, 16, start_load, 0)
    cot_copy = pltpu.make_async_copy(cot_hbm, cot_ref, act_sem.at[16])
    cot_copy.start()


    r_i = lax.broadcasted_iota(jnp.int32, (S_DEV, S_DEV), 0)
    c_i = lax.broadcasted_iota(jnp.int32, (S_DEV, S_DEV), 1)
    rows = jnp.broadcast_to(rows_ref[...].astype(F32), (S_DEV, S_DEV))
    row_col = jnp.sum(jnp.where(r_i == c_i, rows, 0.0), axis=1, keepdims=True)
    tok = lax.broadcasted_iota(jnp.int32, onehot.shape, 1).astype(F32)
    onehot[...] = jnp.where(tok == row_col, 1.0, 0.0).astype(BF16)
    ss[32, :, :] = jnp.zeros((8, HALF), F32)

    pick_s, pick_r = sends(), recvs(4)
    pair_s, pair_r = sends(), recvs(16)
    zb_s, zb_r = sends(), recvs(2)
    rel_s, rel_r = sends(), recvs(4)
    rs1_s, rs1_r = sends(), recvs(8)
    rows2_s, rows2_r = sends(), recvs(4)
    g1_s, g1_r = sends(), recvs()
    g2_s, g2_r = sends(), recvs(4)
    rs2_s, rs2_r = sends(2), recvs(2)
    rs3_s, rs3_r = sends(), recvs()
    rs4_s, rs4_r = sends(), recvs()
    gx_s, gx_r = sends(3), recvs(3)
    gz_s, gz_r = sends(3), recvs(3)
    inv_s, inv_r = sends(2), recvs(2)
    s_s, s_r = sends(), recvs()
    t_s, t_r = sends(), recvs()
    out_s, out_r = sends(), recvs()
    assert sends.used <= SENDS and recvs.used <= RECVS

    def pick_copy(p, uu, vv, k):
        return rcopy(
            picks.at[:, p], r1.at[:, vv, k], pick_s, pick_r + vv, at(dev_uv(uu, v, c))
        )

    def pick_body(i, _):
        p = visit(i)[0]
        act_copy(i, p).wait()
        res = jnp.dot(onehot[...], act[:, columns(p)], preferred_element_type=F32).astype(BF16)
        for zz in range(2):
            picks[zz, p, :, :] = res[:, zz * BLK:(zz + 1) * BLK]
        return 0

    def pick_send(i, _):
        p, uu, vv, k = visit(i)

        @pl.when(k != 0)
        def _():
            pick_copy(p, uu, vv, k).start()

        @pl.when(k == 0)
        def _():
            r1[:, vv, 0, :, :] = picks[:, p, :, :]

        return 0

    def pick_both(i, _):
        pick_body(i, 0)
        return pick_send(i, 0)

    with jax.named_scope("picks"):
        lax.fori_loop(0, PICKS_FIRST, pick_body, 0)
    with jax.named_scope("barrier"):
        pl.semaphore_wait(barrier, 33)
    with jax.named_scope("picks2"):
        lax.fori_loop(0, PICKS_FIRST, pick_send, 0)
        lax.fori_loop(PICKS_FIRST, 16, pick_both, 0)
    cot_copy.wait()
    pg[...] = jnp.dot(onehot[...], cot_ref[...], preferred_element_type=F32).astype(BF16)

    def g1_copy(k):
        return rcopy(pg, g1.at[k], g1_s, g1_r, peer_u(k))

    for k in (2, 1, 3):
        g1_copy(k).start()
    cott[...] = cot_ref[...].T

    def grad_pair(i):
        code = jnp.int32(0)
        for n, (a, b) in enumerate(GRAD_ORDER):
            code = jnp.where(i == n, a * 4 + b, code)
        return wrap(x + lax.div(code, 4)) * 4 + wrap(y + lax.rem(code, 4))

    def pair_copy(i, p):
        return rcopy(buf.at[oc, p], pairs.at[p], pair_s, pair_r + i, peer_c)

    def grad_part(i):
        p = grad_pair(i)
        res = jnp.dot(cott[...], act[:, columns(p)], preferred_element_type=F32)
        for zz in range(2):
            other = lax.rem(zz + z, 2)
            main = pl.ds(pl.multiple_of(MAIN - MAIN * other, 8), MAIN)
            tail = pl.ds(pl.multiple_of(2 * MAIN + TAIL * other, 8), TAIL)
            for h in range(2):
                part = res[h * HALF:(h + 1) * HALF, zz * BLK:(zz + 1) * BLK]
                buf[h, p, main, :] = part[:MAIN]
                buf[h, p, tail, :] = part[MAIN:]
        pair_copy(i, p).start()

    def zb_copy(i, p, group):
        return rcopy(buf.at[c, p, SENT:], zb.at[i], zb_s, zb_r + group, peer_z)

    def pair_sum(i):
        p = grad_pair(i)
        pair_copy(i, p).wait_recv()
        buf[c, p, :, :] = buf[c, p, :, :] + pairs[p, :, :]
        @pl.when(i < 7)
        def _():
            zb_copy(i, p, 0).start()

        @pl.when(i >= 7)
        def _():
            zb_copy(i, p, 1).start()

    def early(i, _):
        grad_part(i)
        return 0

    def late(i, _):
        grad_part(i)
        pair_sum(i - LAG)
        return 0

    def rest(i, _):
        pair_sum(i)
        return 0

    def zb_add(i, _):
        p = grad_pair(i)
        buf[c, p, SENT - TAIL:SENT, :] = buf[c, p, SENT - TAIL:SENT, :] + zb[i, :, :]
        return 0

    UP, DOWN = (2, 1), (3, 0)

    def block(k, m):
        return buf.at[c, pair_of(wrap(u + k), wrap(v + m)), 0:SENT]

    def rel_copy(k, n):
        m = (UP if k == 1 else DOWN)[n]
        return rcopy(block(2, m), rel.at[k // 2, n], rel_s, rel_r + (k // 2) * 2 + n, peer_u(k))

    def rs1_copy(k, m):
        return rcopy(block(k, m), rs1.at[k // 2, m], rs1_s, rs1_r + (k // 2) * 4 + m, peer_u(k))

    with jax.named_scope("grad_a"):
        lax.fori_loop(0, LAG, early, 0)
        lax.fori_loop(LAG, GRAD_SPLIT, late, 0)

    def g2_copy(k):
        return rcopy(g1, g2.at[k], g2_s, g2_r + k, peer_v(k))

    def rows2_copy(k):
        return rcopy(r1.at[:, wrap(v + k)], r2.at[:, k], rows2_s, rows2_r + k, peer_v(k))

    with jax.named_scope("rows1wait"):
        for k in (2, 1, 3):
            wait_got(r1.at[:, wrap(v + k), 1:4], pick_r + wrap(v + k))
            rows2_copy(k).start()
        wait_got(g1.at[1:4], g1_r)
        g1[0, :, :] = pg[...]
        for k in (2, 1, 3):
            g2_copy(k).start()
        wait_got(r1.at[:, v, 1:4], pick_r + v)

    with jax.named_scope("grad_b"):
        lax.fori_loop(GRAD_SPLIT, 16, late, 0)
    with jax.named_scope("grad_c"):
        lax.fori_loop(16 - LAG, 16, rest, 0)
        wait_got(zb.at[0:7], zb_r)
        lax.fori_loop(0, 7, zb_add, 0)
    for n in range(2):
        for k in (1, 3):
            rel_copy(k, n).start()

    def fill_table(i, _):
        xx, yy, zz, _, _, _ = chip(lax.div(i, 2))
        d = dev(xx, yy, zz, lax.rem(i, 2))
        b = jnp.int32(-1)
        for q in range(32):
            b = jnp.where(owner_ref[q] == d, q, b)
        bb = jnp.maximum(b, 0)
        bz = lax.rem(bb + z, 2)
        by = wrap(y - lax.rem(lax.div(bb, 2), 4) + 4)
        bx = wrap(x - lax.div(bb, 8) + 4)
        table[i] = jnp.where(b < 0, 32, bz * 16 + bx * 4 + by)
        return 0

    with jax.named_scope("table"):
        lax.fori_loop(0, 64, fill_table, 0)

    def gx_copy(n):
        return rcopy(gr.at[n], gx.at[n], gx_s + n, gx_r + n, peer_c)

    with jax.named_scope("rows2wait"):
        for zz in range(2):
            gr[zz, :, :] = gram(r1[zz, v, :, :, :].reshape(4 * S_DEV, BLK))
        gr[2, :, :] = gram(g1[...].reshape(4 * S_DEV, BLK))
        for k in (1, 3, 2):
            rows2_copy(k).wait_recv()
            for zz in range(2):
                gr[zz, :, :] += gram(r2[zz, k, :, :, :].reshape(4 * S_DEV, BLK))

    @pl.when(c == 1)
    def _():
        gx_copy(oz).start()
        gx_copy(z).start()

    wait_got(zb.at[7:16], zb_r + 1)
    lax.fori_loop(7, 16, zb_add, 0)
    for n in range(2):
        rs1_copy(1, DOWN[n]).start()
        rs1_copy(3, UP[n]).start()

    def gz_copy(n):
        half = pl.ds(n * HALF, HALF)
        return rcopy(gh.at[half], gz.at[half], gz_s + n, gz_r + n, peer_w if n else peer_z)

    gz_all = rcopy(gh, gz, gz_s + 2, gz_r + 2, peer_z)

    @pl.when(c == 0)
    def _():
        with jax.named_scope("gx"):
            gx_copy(oz).wait_recv()
        gh[...] = gr[oz, :, :] + gx[oz, :, :]
        gz_copy(0).start()
        gz_copy(1).start()
        gx_copy(z).wait_recv()
        m_ref[...] = gr[z, :, :] + gx[z, :, :]

    with jax.named_scope("relay"):
        for n in range(2):
            for k in (1, 3):
                rel_copy(k, n).wait_recv()
                m = (UP if k == 1 else DOWN)[n]
                p = pair_of(wrap(u + k), wrap(v + m))
                buf[c, p, 0:SENT, :] = buf[c, p, 0:SENT, :] + rel[k // 2, n, :, :]
                rs1_copy(k, m).start()

    with jax.named_scope("g2wait"):
        for k in (1, 3, 2):
            g2_copy(k).wait_recv()
            gr[2, :, :] += gram(g2[k, :, :, :].reshape(4 * S_DEV, BLK))

    @pl.when(c == 0)
    def _():
        gx_copy(2).start()

    @pl.when(c == 1)
    def _():
        with jax.named_scope("gxg"):
            gx_copy(2).wait_recv()
        gh[...] = gr[2, :, :] + gx[2, :, :]
        gz_all.start()
        m_ref[...] = gh[...]

    def factor(scale):
        m_ref[...] = (m_ref[...] + gz[...]) * scale + DAMPING * eye(BLK)

    def core1_factor():
        with jax.named_scope("gz"):
            gz_all.wait_recv()
        factor(12.0)

    def s_copy(n):
        xx, yy, zz, dz, dx, dy = chip(n)
        return rcopy(isl.at[zz, xx * 4 + yy], ss.at[n], s_s, s_r, chip_dev(n))

    def s_start(n, _):
        s_copy(n).start()
        return 0

    def rs2_copy(k, part):
        rows = pl.ds(MAIN, HALF) if part else pl.ds(0, MAIN)
        to = rs2b if part else rs2a
        return rcopy(acc1.at[k, rows], to.at[k], rs2_s + part, rs2_r + part, peer_v(k))

    def rs1_finish():
        with jax.named_scope("rs1"):
            for m in (3, 2, 1, 0):
                wait_got(rs1.at[0, m], rs1_r + m)
                wait_got(rs1.at[1, m], rs1_r + 4 + m)
                acc1[m, :, :] = block(0, m)[...] + rs1[0, m, :, :] + rs1[1, m, :, :]
                if m:
                    rs2_copy(m, 0).start()
            for m in (3, 2, 1):
                rs2_copy(m, 1).start()

    half_copy = rcopy(isx, isl, inv_s, inv_r, peer_c)
    ginv_copy = rcopy(x_ref, ginv, inv_s + 1, inv_r + 1, peer_c)

    def t_copy(n):
        return rcopy(dd.at[n], tt.at[n], t_s, t_r, chip_dev(n))

    def t_start(n, _):
        t_copy(n).start()
        return 0

    def slots_back():
        ss[0, :, :] = isl[z, x * 4 + y, :, :]
        with jax.named_scope("s"):
            wait_got(ss.at[1:32], s_r)
        with jax.named_scope("select"):
            for n in range(32):
                for cc in range(2):
                    dd[n, cc, :, :] = ss[table[2 * n + cc], :, :]
            lax.fori_loop(1, 32, t_start, 0)
        tt[0, :, :, :] = dd[0, :, :, :]

    @pl.when(c == 0)
    def _():
        with jax.named_scope("gz"):
            gz_copy(0).wait_recv()
            gz_copy(1).wait_recv()
        factor(1.0 / 4096.0)
        with jax.named_scope("newton_begin"):
            newton_begin(m_ref, x_ref, e_ref)
        with jax.named_scope("newton_end"):
            newton_end(x_ref, e_ref)
        for zz in range(2):
            cols = pl.ds(zz * HALF, HALF)
            isx[zz, :, :, :] = x_ref[HALF:, cols].reshape(16, 8, HALF)
            isl[zz, :, :, :] = x_ref[:HALF, cols].reshape(16, 8, HALF)
        half_copy.start()
        lax.fori_loop(1, 32, s_start, 0)
        rs1_finish()
        slots_back()

    @pl.when(c == 1)
    def _():
        with jax.named_scope("half"):
            half_copy.wait_recv()
        lax.fori_loop(1, 32, s_start, 0)
        rs1_finish()
        core1_factor()
        with jax.named_scope("newton_begin"):
            newton_begin(m_ref, x_ref, e_ref)
        slots_back()
        with jax.named_scope("newton_end"):
            newton_end(x_ref, e_ref)
        ginv_copy.start()

    with jax.named_scope("drain"):
        wait_sent(picks.at[:, 0:12], pick_s)
        wait_sent(buf.at[oc], pair_s)
        wait_sent(zb, zb_s)
        wait_sent(g1.at[1:4], g1_s)
        wait_sent(g2.at[1:4], g2_s)
        wait_sent(r2.at[:, 1:4], rows2_s)
        wait_sent(rel, rel_s)
        wait_sent(rs1, rs1_s)

        @pl.when(c == 0)
        def _():
            for copy in [gx_copy(2), gz_copy(0), gz_copy(1), half_copy]:
                copy.wait_send()

        @pl.when(c == 1)
        def _():
            for copy in [gx_copy(oz), gx_copy(z), gz_all, ginv_copy]:
                copy.wait_send()

    with jax.named_scope("rs2a"):
        wait_got(rs2a.at[1:4], rs2_r)
    acc2[...] = acc1[0, 0:MAIN, :] + rs2a[1, :, :] + rs2a[2, :, :] + rs2a[3, :, :]
    rs3_copy = rcopy(acc2, rs3, rs3_s, rs3_r, peer_z)
    rs3_copy.start()
    with jax.named_scope("rs2b"):
        wait_got(rs2b.at[1:4], rs2_r + 1)
    fin[c, :, :] = acc1[0, MAIN:SENT, :] + rs2b[1, :, :] + rs2b[2, :, :] + rs2b[3, :, :]
    with jax.named_scope("rs3"):
        rs3_copy.wait_recv()
    fin[c, 0:MAIN, :] = fin[c, 0:MAIN, :] + rs3[...]
    rs4_copy = rcopy(fin.at[c], fin.at[c], rs4_s, rs4_r, peer_c)
    rs4_copy.start()

    def assemble(n, _):
        dz, dx, dy = lax.div(n, 16), lax.rem(lax.div(n, 4), 4), lax.rem(n, 4)
        row = wrap(x - dx + 4) * 4 + wrap(y - dy + 4)
        zz = lax.rem(z + dz, 2)
        for cc in range(2):
            outh[cc, 0, zz, row, :, :] = tt[n, cc, :, :]
        return 0

    with jax.named_scope("t"):
        wait_got(tt.at[1:32], t_r)
    lax.fori_loop(0, 32, assemble, 0, unroll=4)
    out_copy = rcopy(outh.at[oc, 0], outh.at[oc, 1], out_s, out_r, peer_c)
    out_copy.start()

    with jax.named_scope("rs4"):
        rs4_copy.wait_recv()

    @pl.when(c == 0)
    def _():
        ginv_copy.wait_recv()

    @pl.when(c == 1)
    def _():
        ginv[...] = x_ref[...]

    with jax.named_scope("final"):
        grad = fin[...].reshape(BLK, BLK)
        nt = (((1,), (1,)), ((), ()))
        left = dot_hi(isl[0, :, :, :].reshape(HALF, HALF), grad[:, :HALF], nt)
        left += dot_hi(isl[1, :, :, :].reshape(HALF, HALF), grad[:, HALF:], nt)
        step_v[...] = dot_hi(left, ginv[...])
    step_copy = pltpu.make_async_copy(step_v, step_hbm, out_sem.at[0])
    step_copy.start()

    with jax.named_scope("outx"):
        out_copy.wait_recv()
    for n in range(2):
        h = (1 - n) * c + n * oc
        for zz in range(2):
            slot_v[h, :, zz * HALF:(zz + 1) * HALF] = outh[c, n, zz, :, :, :].reshape(HALF, HALF)
    slot_copy = pltpu.make_async_copy(slot_v, slot_hbm, out_sem.at[1])
    slot_copy.start()

    with jax.named_scope("drain2"):
        wait_sent(ss.at[1:32], s_s)
        wait_sent(tt.at[1:32], t_s)
        wait_sent(rs2a.at[1:4], rs2_s)
        wait_sent(rs2b.at[1:4], rs2_s + 1)
        for copy in [rs3_copy, rs4_copy, out_copy]:
            copy.wait_send()
    with jax.named_scope("store"):
        step_copy.wait()
        slot_copy.wait()


def settle(step_in, slot_in, step_out, slot_out):
    step_out[...] = step_in[...]
    slot_out[...] = slot_in[...]


def per_device(activations, cotangent, sampled_rows, block_owner):
    tokens, width = activations.shape
    vmem = pltpu.VMEM
    step, slot = pl.pallas_call(
        kernel,
        out_shape=(
            jax.ShapeDtypeStruct((HALF, BLK), F32),
            jax.ShapeDtypeStruct((2, HALF, BLK), F32),
        ),
        in_specs=[
            pl.BlockSpec(memory_space=pl.ANY),
            pl.BlockSpec(memory_space=pl.ANY),
            pl.BlockSpec(memory_space=pltpu.VMEM),
            pl.BlockSpec(memory_space=pltpu.SMEM),
        ],
        out_specs=(
            pl.BlockSpec(memory_space=pl.ANY),
            pl.BlockSpec(memory_space=pl.ANY),
        ),
        scratch_shapes=[
            vmem((tokens, width), BF16),
            vmem((tokens, BLK), BF16),
            vmem((BLK, tokens), BF16),
            vmem((S_DEV, tokens), BF16),
            vmem((2, 16, BLK, BLK), F32),
            vmem((16, BLK, BLK), F32),
            vmem((16, TAIL, BLK), F32),
            vmem((2, 2, SENT, BLK), F32),
            vmem((2, 4, SENT, BLK), F32),
            vmem((4, SENT, BLK), F32),
            vmem((4, MAIN, BLK), F32),
            vmem((4, HALF, BLK), F32),
            vmem((MAIN, BLK), F32),
            vmem((MAIN, BLK), F32),
            vmem((2, HALF, BLK), F32),
            vmem((2, 16, S_DEV, BLK), BF16),
            vmem((S_DEV, BLK), BF16),
            vmem((2, 4, 4, S_DEV, BLK), BF16),
            vmem((2, 4, 4, S_DEV, BLK), BF16),
            vmem((4, S_DEV, BLK), BF16),
            vmem((4, 4, S_DEV, BLK), BF16),
            vmem((3, BLK, BLK), F32),
            vmem((3, BLK, BLK), F32),
            vmem((BLK, BLK), F32),
            vmem((BLK, BLK), F32),
            vmem((BLK, BLK), F32),
            vmem((BLK, BLK), F32),
            vmem((BLK, BLK), F32),
            vmem((2, 16, 8, HALF), F32),
            vmem((2, 16, 8, HALF), F32),
            vmem((BLK, BLK), F32),
            vmem((33, 8, HALF), F32),
            vmem((32, 2, 8, HALF), F32),
            vmem((32, 2, 8, HALF), F32),
            vmem((2, 2, 2, 16, 8, HALF), F32),
            vmem((2, HALF, BLK), F32),
            vmem((HALF, BLK), F32),
            pltpu.SMEM((64,), jnp.int32),
            pltpu.SemaphoreType.DMA((17,)),
            pltpu.SemaphoreType.DMA((2,)),
            pltpu.SemaphoreType.DMA((SENDS,)),
            pltpu.SemaphoreType.DMA((RECVS,)),
        ],
        compiler_params=pltpu.CompilerParams(
            collective_id=0, has_side_effects=True, vmem_limit_bytes=60 * 1024 * 1024
        ),
    )(activations, cotangent, sampled_rows.reshape(1, S_DEV), block_owner)
    step, slot = pl.pallas_call(
        settle,
        out_shape=(
            jax.ShapeDtypeStruct((HALF, BLK), F32),
            jax.ShapeDtypeStruct((2, HALF, BLK), F32),
        ),
    )(step, slot)
    return step, slot.reshape(1, BLK, BLK)


def solution(mesh):
    return jax.shard_map(
        per_device,
        mesh=mesh,
        in_specs=(P("dp", None), P("dp", "tensor"), P("dp"), P()),
        out_specs=(P("dp", "tensor"), P("dp", None, None)),
        check_vma=False,
    )
```

```python
import jax
import jax.numpy as jnp
from jax import lax
from jax.experimental import pallas as pl
from jax.experimental.pallas import tpu as pltpu
from jax.sharding import PartitionSpec as P

S_DEV = 64
BLK = 256
HALF = 128
ITERS = 10
DAMPING = 0.05
MESH = pl.DeviceIdType.MESH
HI = lax.Precision.HIGHEST
F32 = jnp.float32
BF16 = jnp.bfloat16


class Sems:
    def __init__(self):
        self.used = 0

    def __call__(self, count=1):
        base = self.used
        self.used += count
        return base


SENDS = 24
RECVS = 64
LAG = 3
LOADS_FIRST = 3
GRAD_SPLIT = 11
PICKS_FIRST = 8
TAIL = 32
MAIN = HALF - TAIL
SENT = BLK - TAIL
GRAD_ORDER = (
    (2, 2), (2, 1), (1, 2), (2, 3), (3, 2), (2, 0), (0, 2),
    (1, 1), (1, 3), (3, 1), (3, 3), (1, 0), (0, 1), (3, 0), (0, 3), (0, 0),
)


def dot_hi(a, b, dims=(((1,), (0,)), ((), ()))):
    return lax.dot_general(a, b, dims, precision=HI, preferred_element_type=F32)


def gram(rows):
    return lax.dot_general(rows, rows, (((0,), (0,)), ((), ())), preferred_element_type=F32)


def eye(n):
    r = lax.broadcasted_iota(jnp.int32, (n, n), 0)
    c = lax.broadcasted_iota(jnp.int32, (n, n), 1)
    return jnp.where(r == c, 1.0, 0.0).astype(F32)


def newton_step(x_ref, e_ref):
    def step(k, _):
        e = e_ref[...]
        x = x_ref[...]
        both = dot_hi(jnp.concatenate([x, e], axis=0), e)
        x_ref[...] = x + both[:BLK]
        e_ref[...] = both[BLK:]
        return 0

    return step


def newton_begin(m_ref, x_ref, e_ref):
    ident = eye(BLK)
    m = m_ref[...]
    bound = jnp.max(jnp.sum(jnp.abs(m), axis=1, keepdims=True), axis=0, keepdims=True)
    inv = 1.0 / bound
    e = ident - m * inv
    x_ref[...] = (ident + e) * inv
    e_ref[...] = dot_hi(e, e)
    lax.fori_loop(0, 4, newton_step(x_ref, e_ref), 0)
    e_ref[...] = ident - dot_hi(m, x_ref[...])


def newton_end(x_ref, e_ref):
    lax.fori_loop(0, 4, newton_step(x_ref, e_ref), 0)
    x_ref[...] += dot_hi(x_ref[...], e_ref[...])


def kernel(
    act_hbm, cot_hbm, rows_ref, owner_ref,
    step_hbm, slot_hbm,
    act, cot_ref, cott, onehot, buf, pairs, zb, rel, rs1, acc1, rs2a, rs2b, acc2, rs3, fin,
    picks, pg, r1, r2, g1, g2,
    gr, gx, gh, gz, m_ref, x_ref, e_ref, isl, isx, ginv,
    ss, dd, tt, outh, slot_v, step_v, table,
    act_sem, out_sem, send_sem, recv_sem,
):
    dp = lax.axis_index("dp")
    ten = lax.axis_index("tensor")
    c = lax.rem(dp, 2)
    z = lax.rem(lax.div(dp, 2), 2)
    y = lax.rem(lax.div(dp, 4), 4)
    x = lax.div(dp, 16)
    u = (1 - c) * x + c * y
    v = (1 - c) * y + c * x
    oc = 1 - c
    oz = 1 - z

    def wrap(a):
        return lax.rem(a, 4)

    def dev(xx, yy, zz, cc):
        return ((xx * 4 + yy) * 2 + zz) * 2 + cc

    def dev_uv(uu, vv, cc):
        return dev((1 - c) * uu + c * vv, (1 - c) * vv + c * uu, z, cc)

    def at(d):
        return {"dp": d, "tensor": ten}

    def peer_u(k):
        return at(dev_uv(wrap(u + k), v, c))

    def peer_v(k):
        return at(dev_uv(u, wrap(v + k), c))

    peer_z = at(dev(x, y, oz, c))
    peer_w = {"dp": dev(x, y, oz, c), "tensor": wrap(ten + 3 + 2 * z)}
    peer_c = at(dev(x, y, z, oc))

    def pair_of(uu, vv):
        return (1 - c) * (uu * 4 + vv) + c * (vv * 4 + uu)

    sends, recvs = Sems(), Sems()

    def rcopy(src, dst, send_i, recv_i, to):
        return pltpu.make_async_remote_copy(
            src_ref=src, dst_ref=dst, send_sem=send_sem.at[send_i], recv_sem=recv_sem.at[recv_i],
            device_id=to, device_id_type=MESH,
        )

    def wait_sent(ref, send_i):
        rcopy(ref, ref, send_i, 0, peer_c).wait_send()

    def wait_got(ref, recv_i):
        rcopy(ref, ref, 0, recv_i, peer_c).wait_recv()

    def columns(p):
        return pl.ds(pl.multiple_of(p * 2 * BLK, 2 * BLK), 2 * BLK)

    def act_copy(i, p):
        return pltpu.make_async_copy(act_hbm.at[:, columns(p)], act.at[:, columns(p)], act_sem.at[i])

    def visit(i):
        g = wrap(x + wrap(lax.div(i, 4) + 1))
        j = wrap(y + wrap(lax.rem(i, 4) + 1))
        uu = (1 - c) * g + c * j
        vv = (1 - c) * j + c * g
        return g * 4 + j, uu, vv, wrap(uu - u + 4)

    def start_load(i, _):
        act_copy(i, visit(i)[0]).start()
        return 0

    lax.fori_loop(0, LOADS_FIRST, start_load, 0)
    barrier = pltpu.get_barrier_semaphore()

    def chip(n):
        if isinstance(n, int):
            dz, dx, dy = n // 16, n // 4 % 4, n % 4
        else:
            dz, dx, dy = lax.div(n, 16), lax.rem(lax.div(n, 4), 4), lax.rem(n, 4)
        xx, yy, zz = wrap(x + dx), wrap(y + dy), lax.rem(z + dz, 2)
        return xx, yy, zz, dz, dx, dy

    def chip_dev(n):
        xx, yy, zz, dz, dx, dy = chip(n)
        other = dz * ((dx + dy) % 2)
        return {"dp": dev(xx, yy, zz, c), "tensor": wrap(ten + other * (3 + 2 * z))}

    for n in range(31, 0, -1):
        pl.semaphore_signal(barrier, inc=1, device_id=chip_dev(n), device_id_type=MESH)
    for to in [peer_w, peer_c]:
        pl.semaphore_signal(barrier, inc=1, device_id=to, device_id_type=MESH)
    lax.fori_loop(LOADS_FIRST, 16, start_load, 0)
    cot_copy = pltpu.make_async_copy(cot_hbm, cot_ref, act_sem.at[16])
    cot_copy.start()


    r_i = lax.broadcasted_iota(jnp.int32, (S_DEV, S_DEV), 0)
    c_i = lax.broadcasted_iota(jnp.int32, (S_DEV, S_DEV), 1)
    rows = jnp.broadcast_to(rows_ref[...].astype(F32), (S_DEV, S_DEV))
    row_col = jnp.sum(jnp.where(r_i == c_i, rows, 0.0), axis=1, keepdims=True)
    tok = lax.broadcasted_iota(jnp.int32, onehot.shape, 1).astype(F32)
    onehot[...] = jnp.where(tok == row_col, 1.0, 0.0).astype(BF16)
    ss[32, :, :] = jnp.zeros((8, HALF), F32)

    pick_s, pick_r = sends(), recvs(4)
    pair_s, pair_r = sends(), recvs(16)
    zb_s, zb_r = sends(), recvs(2)
    rel_s, rel_r = sends(), recvs(4)
    rs1_s, rs1_r = sends(), recvs(8)
    rows2_s, rows2_r = sends(), recvs(4)
    g1_s, g1_r = sends(), recvs()
    g2_s, g2_r = sends(), recvs(4)
    rs2_s, rs2_r = sends(2), recvs(2)
    rs3_s, rs3_r = sends(), recvs()
    rs4_s, rs4_r = sends(), recvs()
    gx_s, gx_r = sends(3), recvs(3)
    gz_s, gz_r = sends(3), recvs(3)
    inv_s, inv_r = sends(2), recvs(2)
    s_s, s_r = sends(), recvs()
    t_s, t_r = sends(), recvs()
    out_s, out_r = sends(), recvs()
    assert sends.used <= SENDS and recvs.used <= RECVS

    def pick_copy(p, uu, vv, k):
        return rcopy(
            picks.at[:, p], r1.at[:, vv, k], pick_s, pick_r + vv, at(dev_uv(uu, v, c))
        )

    def pick_body(i, _):
        p = visit(i)[0]
        act_copy(i, p).wait()
        res = jnp.dot(onehot[...], act[:, columns(p)], preferred_element_type=F32).astype(BF16)
        for zz in range(2):
            picks[zz, p, :, :] = res[:, zz * BLK:(zz + 1) * BLK]
        return 0

    def pick_send(i, _):
        p, uu, vv, k = visit(i)

        @pl.when(k != 0)
        def _():
            pick_copy(p, uu, vv, k).start()

        @pl.when(k == 0)
        def _():
            r1[:, vv, 0, :, :] = picks[:, p, :, :]

        return 0

    def pick_both(i, _):
        pick_body(i, 0)
        return pick_send(i, 0)

    with jax.named_scope("picks"):
        lax.fori_loop(0, PICKS_FIRST, pick_body, 0)
    with jax.named_scope("barrier"):
        pl.semaphore_wait(barrier, 33)
    with jax.named_scope("picks2"):
        lax.fori_loop(0, PICKS_FIRST, pick_send, 0)
        lax.fori_loop(PICKS_FIRST, 16, pick_both, 0)
    cot_copy.wait()
    pg[...] = jnp.dot(onehot[...], cot_ref[...], preferred_element_type=F32).astype(BF16)

    def g1_copy(k):
        return rcopy(pg, g1.at[k], g1_s, g1_r, peer_u(k))

    for k in (2, 1, 3):
        g1_copy(k).start()
    cott[...] = cot_ref[...].T

    def grad_pair(i):
        code = jnp.int32(0)
        for n, (a, b) in enumerate(GRAD_ORDER):
            code = jnp.where(i == n, a * 4 + b, code)
        return wrap(x + lax.div(code, 4)) * 4 + wrap(y + lax.rem(code, 4))

    def pair_copy(i, p):
        return rcopy(buf.at[oc, p], pairs.at[p], pair_s, pair_r + i, peer_c)

    def grad_part(i):
        p = grad_pair(i)
        res = jnp.dot(cott[...], act[:, columns(p)], preferred_element_type=F32)
        for zz in range(2):
            other = lax.rem(zz + z, 2)
            main = pl.ds(pl.multiple_of(MAIN - MAIN * other, 8), MAIN)
            tail = pl.ds(pl.multiple_of(2 * MAIN + TAIL * other, 8), TAIL)
            for h in range(2):
                part = res[h * HALF:(h + 1) * HALF, zz * BLK:(zz + 1) * BLK]
                buf[h, p, main, :] = part[:MAIN]
                buf[h, p, tail, :] = part[MAIN:]
        pair_copy(i, p).start()

    def zb_copy(i, p, group):
        return rcopy(buf.at[c, p, SENT:], zb.at[i], zb_s, zb_r + group, peer_z)

    def pair_sum(i):
        p = grad_pair(i)
        pair_copy(i, p).wait_recv()
        buf[c, p, :, :] = buf[c, p, :, :] + pairs[p, :, :]
        @pl.when(i < 7)
        def _():
            zb_copy(i, p, 0).start()

        @pl.when(i >= 7)
        def _():
            zb_copy(i, p, 1).start()

    def early(i, _):
        grad_part(i)
        return 0

    def late(i, _):
        grad_part(i)
        pair_sum(i - LAG)
        return 0

    def rest(i, _):
        pair_sum(i)
        return 0

    def zb_add(i, _):
        p = grad_pair(i)
        buf[c, p, SENT - TAIL:SENT, :] = buf[c, p, SENT - TAIL:SENT, :] + zb[i, :, :]
        return 0

    UP, DOWN = (2, 1), (3, 0)

    def block(k, m):
        return buf.at[c, pair_of(wrap(u + k), wrap(v + m)), 0:SENT]

    def rel_copy(k, n):
        m = (UP if k == 1 else DOWN)[n]
        return rcopy(block(2, m), rel.at[k // 2, n], rel_s, rel_r + (k // 2) * 2 + n, peer_u(k))

    def rs1_copy(k, m):
        return rcopy(block(k, m), rs1.at[k // 2, m], rs1_s, rs1_r + (k // 2) * 4 + m, peer_u(k))

    with jax.named_scope("grad_a"):
        lax.fori_loop(0, LAG, early, 0)
        lax.fori_loop(LAG, GRAD_SPLIT, late, 0)

    def g2_copy(k):
        return rcopy(g1, g2.at[k], g2_s, g2_r + k, peer_v(k))

    def rows2_copy(k):
        return rcopy(r1.at[:, wrap(v + k)], r2.at[:, k], rows2_s, rows2_r + k, peer_v(k))

    with jax.named_scope("rows1wait"):
        for k in (2, 1, 3):
            wait_got(r1.at[:, wrap(v + k), 1:4], pick_r + wrap(v + k))
            rows2_copy(k).start()
        wait_got(g1.at[1:4], g1_r)
        g1[0, :, :] = pg[...]
        for k in (2, 1, 3):
            g2_copy(k).start()
        wait_got(r1.at[:, v, 1:4], pick_r + v)

    with jax.named_scope("grad_b"):
        lax.fori_loop(GRAD_SPLIT, 16, late, 0)
    with jax.named_scope("grad_c"):
        lax.fori_loop(16 - LAG, 16, rest, 0)
        wait_got(zb.at[0:7], zb_r)
        lax.fori_loop(0, 7, zb_add, 0)
    for n in range(2):
        for k in (1, 3):
            rel_copy(k, n).start()

    def gx_copy(n):
        return rcopy(gr.at[n], gx.at[n], gx_s + n, gx_r + n, peer_c)

    with jax.named_scope("rows2wait"):
        for zz in range(2):
            gr[zz, :, :] = gram(r1[zz, v, :, :, :].reshape(4 * S_DEV, BLK))
        gr[2, :, :] = gram(g1[...].reshape(4 * S_DEV, BLK))
        for k in (1, 3, 2):
            rows2_copy(k).wait_recv()
            for zz in range(2):
                gr[zz, :, :] += gram(r2[zz, k, :, :, :].reshape(4 * S_DEV, BLK))

    @pl.when(c == 1)
    def _():
        gx_copy(oz).start()
        gx_copy(z).start()

    wait_got(zb.at[7:16], zb_r + 1)
    lax.fori_loop(7, 16, zb_add, 0)
    for n in range(2):
        rs1_copy(1, DOWN[n]).start()
        rs1_copy(3, UP[n]).start()

    def gz_copy(n):
        half = pl.ds(n * HALF, HALF)
        return rcopy(gh.at[half], gz.at[half], gz_s + n, gz_r + n, peer_w if n else peer_z)

    gz_all = rcopy(gh, gz, gz_s + 2, gz_r + 2, peer_z)

    @pl.when(c == 0)
    def _():
        with jax.named_scope("gx"):
            gx_copy(oz).wait_recv()
        gh[...] = gr[oz, :, :] + gx[oz, :, :]
        gz_copy(0).start()
        gz_copy(1).start()
        gx_copy(z).wait_recv()
        m_ref[...] = gr[z, :, :] + gx[z, :, :]

    def fill_table(i, _):
        xx, yy, zz, _, _, _ = chip(lax.div(i, 2))
        d = dev(xx, yy, zz, lax.rem(i, 2))
        b = jnp.int32(-1)
        for q in range(32):
            b = jnp.where(owner_ref[q] == d, q, b)
        bb = jnp.maximum(b, 0)
        bz = lax.rem(bb + z, 2)
        by = wrap(y - lax.rem(lax.div(bb, 2), 4) + 4)
        bx = wrap(x - lax.div(bb, 8) + 4)
        table[i] = jnp.where(b < 0, 32, bz * 16 + bx * 4 + by)
        return 0

    with jax.named_scope("table"):
        lax.fori_loop(0, 64, fill_table, 0)

    with jax.named_scope("g2wait"):
        for k in (1, 3, 2):
            g2_copy(k).wait_recv()
            gr[2, :, :] += gram(g2[k, :, :, :].reshape(4 * S_DEV, BLK))

    @pl.when(c == 0)
    def _():
        gx_copy(2).start()

    @pl.when(c == 1)
    def _():
        with jax.named_scope("gxg"):
            gx_copy(2).wait_recv()
        gh[...] = gr[2, :, :] + gx[2, :, :]
        gz_all.start()
        m_ref[...] = gh[...]

    def relay():
        with jax.named_scope("relay"):
            for n in range(2):
                for k in (1, 3):
                    rel_copy(k, n).wait_recv()
                    m = (UP if k == 1 else DOWN)[n]
                    p = pair_of(wrap(u + k), wrap(v + m))
                    buf[c, p, 0:SENT, :] = buf[c, p, 0:SENT, :] + rel[k // 2, n, :, :]
                    rs1_copy(k, m).start()

    relay()

    def factor(scale):
        m_ref[...] = (m_ref[...] + gz[...]) * scale + DAMPING * eye(BLK)

    def core1_factor():
        with jax.named_scope("gz"):
            gz_all.wait_recv()
        factor(12.0)

    def s_copy(n):
        xx, yy, zz, dz, dx, dy = chip(n)
        return rcopy(isl.at[zz, xx * 4 + yy], ss.at[n], s_s, s_r, chip_dev(n))

    def s_start():
        for n in range(31, 0, -1):
            s_copy(n).start()

    def rs2_copy(k, part):
        rows = pl.ds(MAIN, HALF) if part else pl.ds(0, MAIN)
        to = rs2b if part else rs2a
        return rcopy(acc1.at[k, rows], to.at[k], rs2_s + part, rs2_r + part, peer_v(k))

    def rs1_finish():
        with jax.named_scope("rs1"):
            for m in (3, 2, 1, 0):
                wait_got(rs1.at[0, m], rs1_r + m)
                wait_got(rs1.at[1, m], rs1_r + 4 + m)
                acc1[m, :, :] = block(0, m)[...] + rs1[0, m, :, :] + rs1[1, m, :, :]
                if m:
                    rs2_copy(m, 0).start()
            for m in (3, 2, 1):
                rs2_copy(m, 1).start()

    half_copy = rcopy(isx, isl, inv_s, inv_r, peer_c)
    ginv_copy = rcopy(x_ref, ginv, inv_s + 1, inv_r + 1, peer_c)

    def t_copy(n):
        return rcopy(dd.at[n], tt.at[n], t_s, t_r, chip_dev(n))

    def slots_back():
        ss[0, :, :] = isl[z, x * 4 + y, :, :]
        with jax.named_scope("s"):
            wait_got(ss.at[1:32], s_r)
        with jax.named_scope("select"):
            for n in range(31, -1, -1):
                for cc in range(2):
                    dd[n, cc, :, :] = ss[table[2 * n + cc], :, :]
                if n:
                    t_copy(n).start()
        tt[0, :, :, :] = dd[0, :, :, :]

    @pl.when(c == 0)
    def _():
        with jax.named_scope("gz"):
            gz_copy(0).wait_recv()
            gz_copy(1).wait_recv()
        factor(1.0 / 4096.0)
        with jax.named_scope("newton_begin"):
            newton_begin(m_ref, x_ref, e_ref)
        with jax.named_scope("newton_end"):
            newton_end(x_ref, e_ref)
        for zz in range(2):
            cols = pl.ds(zz * HALF, HALF)
            isx[zz, :, :, :] = x_ref[HALF:, cols].reshape(16, 8, HALF)
            isl[zz, :, :, :] = x_ref[:HALF, cols].reshape(16, 8, HALF)
        half_copy.start()
        s_start()
        rs1_finish()
        slots_back()

    @pl.when(c == 1)
    def _():
        core1_factor()
        with jax.named_scope("newton_begin"):
            newton_begin(m_ref, x_ref, e_ref)
        with jax.named_scope("half"):
            half_copy.wait_recv()
        s_start()
        rs1_finish()
        with jax.named_scope("newton_end"):
            newton_end(x_ref, e_ref)
        ginv_copy.start()
        slots_back()

    with jax.named_scope("drain"):
        wait_sent(picks.at[:, 0:12], pick_s)
        wait_sent(buf.at[oc], pair_s)
        wait_sent(zb, zb_s)
        wait_sent(g1.at[1:4], g1_s)
        wait_sent(g2.at[1:4], g2_s)
        wait_sent(r2.at[:, 1:4], rows2_s)
        wait_sent(rel, rel_s)
        wait_sent(rs1, rs1_s)

        @pl.when(c == 0)
        def _():
            for copy in [gx_copy(2), gz_copy(0), gz_copy(1), half_copy]:
                copy.wait_send()

        @pl.when(c == 1)
        def _():
            for copy in [gx_copy(oz), gx_copy(z), gz_all]:
                copy.wait_send()

    with jax.named_scope("rs2a"):
        wait_got(rs2a.at[1:4], rs2_r)
    acc2[...] = acc1[0, 0:MAIN, :] + rs2a[1, :, :] + rs2a[2, :, :] + rs2a[3, :, :]
    rs3_copy = rcopy(acc2, rs3, rs3_s, rs3_r, peer_z)
    rs3_copy.start()
    with jax.named_scope("rs2b"):
        wait_got(rs2b.at[1:4], rs2_r + 1)
    fin[c, :, :] = acc1[0, MAIN:SENT, :] + rs2b[1, :, :] + rs2b[2, :, :] + rs2b[3, :, :]
    with jax.named_scope("rs3"):
        rs3_copy.wait_recv()
    fin[c, 0:MAIN, :] = fin[c, 0:MAIN, :] + rs3[...]
    rs4_copy = rcopy(fin.at[c], fin.at[c], rs4_s, rs4_r, peer_c)
    rs4_copy.start()

    def assemble(n, _):
        dz, dx, dy = lax.div(n, 16), lax.rem(lax.div(n, 4), 4), lax.rem(n, 4)
        row = wrap(x - dx + 4) * 4 + wrap(y - dy + 4)
        zz = lax.rem(z + dz, 2)
        for cc in range(2):
            outh[cc, 0, zz, row, :, :] = tt[n, cc, :, :]
        return 0

    with jax.named_scope("t"):
        wait_got(tt.at[1:32], t_r)
    lax.fori_loop(0, 32, assemble, 0, unroll=4)
    out_copy = rcopy(outh.at[oc, 0], outh.at[oc, 1], out_s, out_r, peer_c)
    out_copy.start()

    with jax.named_scope("rs4"):
        rs4_copy.wait_recv()

    @pl.when(c == 0)
    def _():
        ginv_copy.wait_recv()

    @pl.when(c == 1)
    def _():
        ginv[...] = x_ref[...]

    with jax.named_scope("final"):
        grad = fin[...].reshape(BLK, BLK)
        nt = (((1,), (1,)), ((), ()))
        left = dot_hi(isl[0, :, :, :].reshape(HALF, HALF), grad[:, :HALF], nt)
        left += dot_hi(isl[1, :, :, :].reshape(HALF, HALF), grad[:, HALF:], nt)
        step_v[...] = dot_hi(left, ginv[...])
    step_copy = pltpu.make_async_copy(step_v, step_hbm, out_sem.at[0])
    step_copy.start()

    with jax.named_scope("outx"):
        out_copy.wait_recv()
    for n in range(2):
        h = (1 - n) * c + n * oc
        for zz in range(2):
            slot_v[h, :, zz * HALF:(zz + 1) * HALF] = outh[c, n, zz, :, :, :].reshape(HALF, HALF)
    slot_copy = pltpu.make_async_copy(slot_v, slot_hbm, out_sem.at[1])
    slot_copy.start()

    with jax.named_scope("drain2"):
        wait_sent(ss.at[1:32], s_s)
        wait_sent(tt.at[1:32], t_s)
        wait_sent(rs2a.at[1:4], rs2_s)
        wait_sent(rs2b.at[1:4], rs2_s + 1)
        for copy in [rs3_copy, rs4_copy, out_copy]:
            copy.wait_send()

        @pl.when(c == 1)
        def _():
            ginv_copy.wait_send()

    with jax.named_scope("store"):
        step_copy.wait()
        slot_copy.wait()


def settle(step_in, slot_in, step_out, slot_out):
    step_out[...] = step_in[...]
    slot_out[...] = slot_in[...]


def per_device(activations, cotangent, sampled_rows, block_owner):
    tokens, width = activations.shape
    vmem = pltpu.VMEM
    step, slot = pl.pallas_call(
        kernel,
        out_shape=(
            jax.ShapeDtypeStruct((HALF, BLK), F32),
            jax.ShapeDtypeStruct((2, HALF, BLK), F32),
        ),
        in_specs=[
            pl.BlockSpec(memory_space=pl.ANY),
            pl.BlockSpec(memory_space=pl.ANY),
            pl.BlockSpec(memory_space=pltpu.VMEM),
            pl.BlockSpec(memory_space=pltpu.SMEM),
        ],
        out_specs=(
            pl.BlockSpec(memory_space=pl.ANY),
            pl.BlockSpec(memory_space=pl.ANY),
        ),
        scratch_shapes=[
            vmem((tokens, width), BF16),
            vmem((tokens, BLK), BF16),
            vmem((BLK, tokens), BF16),
            vmem((S_DEV, tokens), BF16),
            vmem((2, 16, BLK, BLK), F32),
            vmem((16, BLK, BLK), F32),
            vmem((16, TAIL, BLK), F32),
            vmem((2, 2, SENT, BLK), F32),
            vmem((2, 4, SENT, BLK), F32),
            vmem((4, SENT, BLK), F32),
            vmem((4, MAIN, BLK), F32),
            vmem((4, HALF, BLK), F32),
            vmem((MAIN, BLK), F32),
            vmem((MAIN, BLK), F32),
            vmem((2, HALF, BLK), F32),
            vmem((2, 16, S_DEV, BLK), BF16),
            vmem((S_DEV, BLK), BF16),
            vmem((2, 4, 4, S_DEV, BLK), BF16),
            vmem((2, 4, 4, S_DEV, BLK), BF16),
            vmem((4, S_DEV, BLK), BF16),
            vmem((4, 4, S_DEV, BLK), BF16),
            vmem((3, BLK, BLK), F32),
            vmem((3, BLK, BLK), F32),
            vmem((BLK, BLK), F32),
            vmem((BLK, BLK), F32),
            vmem((BLK, BLK), F32),
            vmem((BLK, BLK), F32),
            vmem((BLK, BLK), F32),
            vmem((2, 16, 8, HALF), F32),
            vmem((2, 16, 8, HALF), F32),
            vmem((BLK, BLK), F32),
            vmem((33, 8, HALF), F32),
            vmem((32, 2, 8, HALF), F32),
            vmem((32, 2, 8, HALF), F32),
            vmem((2, 2, 2, 16, 8, HALF), F32),
            vmem((2, HALF, BLK), F32),
            vmem((HALF, BLK), F32),
            pltpu.SMEM((64,), jnp.int32),
            pltpu.SemaphoreType.DMA((17,)),
            pltpu.SemaphoreType.DMA((2,)),
            pltpu.SemaphoreType.DMA((SENDS,)),
            pltpu.SemaphoreType.DMA((RECVS,)),
        ],
        compiler_params=pltpu.CompilerParams(
            collective_id=0, has_side_effects=True, vmem_limit_bytes=60 * 1024 * 1024
        ),
    )(activations, cotangent, sampled_rows.reshape(1, S_DEV), block_owner)
    step, slot = pl.pallas_call(
        settle,
        out_shape=(
            jax.ShapeDtypeStruct((HALF, BLK), F32),
            jax.ShapeDtypeStruct((2, HALF, BLK), F32),
        ),
    )(step, slot)
    return step, slot.reshape(1, BLK, BLK)


def solution(mesh):
    return jax.shard_map(
        per_device,
        mesh=mesh,
        in_specs=(P("dp", None), P("dp", "tensor"), P("dp"), P()),
        out_specs=(P("dp", "tensor"), P("dp", None, None)),
        check_vma=False,
    )
```

```python
import jax
import jax.numpy as jnp
from jax import lax
from jax.experimental import pallas as pl
from jax.experimental.pallas import tpu as pltpu
from jax.sharding import PartitionSpec as P

S_DEV = 64
BLK = 256
HALF = 128
ITERS = 10
DAMPING = 0.05
MESH = pl.DeviceIdType.MESH
HI = lax.Precision.HIGHEST
F32 = jnp.float32
BF16 = jnp.bfloat16


class Sems:
    def __init__(self):
        self.used = 0

    def __call__(self, count=1):
        base = self.used
        self.used += count
        return base


SENDS = 24
RECVS = 64
LAG = 3
LOADS_FIRST = 3
GRAD_SPLIT = 11
PICKS_FIRST = 8
TAIL = 32
MAIN = HALF - TAIL
SENT = BLK - TAIL
GRAD_ORDER = (
    (2, 2), (2, 1), (1, 2), (2, 3), (3, 2), (2, 0), (0, 2),
    (1, 1), (1, 3), (3, 1), (3, 3), (1, 0), (0, 1), (3, 0), (0, 3), (0, 0),
)


def dot_hi(a, b, dims=(((1,), (0,)), ((), ()))):
    return lax.dot_general(a, b, dims, precision=HI, preferred_element_type=F32)


def gram(rows):
    return lax.dot_general(rows, rows, (((0,), (0,)), ((), ())), preferred_element_type=F32)


def eye(n):
    r = lax.broadcasted_iota(jnp.int32, (n, n), 0)
    c = lax.broadcasted_iota(jnp.int32, (n, n), 1)
    return jnp.where(r == c, 1.0, 0.0).astype(F32)


def newton_step(x_ref, e_ref):
    def step(k, _):
        e = e_ref[...]
        x = x_ref[...]
        both = dot_hi(jnp.concatenate([x, e], axis=0), e)
        x_ref[...] = x + both[:BLK]
        e_ref[...] = both[BLK:]
        return 0

    return step


def newton_begin(m_ref, x_ref, e_ref):
    ident = eye(BLK)
    m = m_ref[...]
    bound = jnp.max(jnp.sum(jnp.abs(m), axis=1, keepdims=True), axis=0, keepdims=True)
    inv = 1.0 / bound
    e = ident - m * inv
    x_ref[...] = (ident + e) * inv
    e_ref[...] = dot_hi(e, e)
    lax.fori_loop(0, 4, newton_step(x_ref, e_ref), 0)
    e_ref[...] = ident - dot_hi(m, x_ref[...])


def newton_end(x_ref, e_ref):
    lax.fori_loop(0, 4, newton_step(x_ref, e_ref), 0)
    x_ref[...] += dot_hi(x_ref[...], e_ref[...])


def kernel(
    act_hbm, cot_hbm, rows_ref, owner_ref,
    step_hbm, slot_hbm,
    act, cot_ref, cott, onehot, buf, pairs, zb, rel, rs1, acc1, rs2a, rs2b, acc2, rs3, fin,
    picks, pg, r1, r2, g1, g2,
    gr, gx, gh, gz, m_ref, x_ref, e_ref, isl, isx, ginv,
    ss, dd, tt, outh, slot_v, step_v, table,
    act_sem, out_sem, send_sem, recv_sem,
):
    dp = lax.axis_index("dp")
    ten = lax.axis_index("tensor")
    c = lax.rem(dp, 2)
    z = lax.rem(lax.div(dp, 2), 2)
    y = lax.rem(lax.div(dp, 4), 4)
    x = lax.div(dp, 16)
    u = (1 - c) * x + c * y
    v = (1 - c) * y + c * x
    oc = 1 - c
    oz = 1 - z

    def wrap(a):
        return lax.rem(a, 4)

    def dev(xx, yy, zz, cc):
        return ((xx * 4 + yy) * 2 + zz) * 2 + cc

    def dev_uv(uu, vv, cc):
        return dev((1 - c) * uu + c * vv, (1 - c) * vv + c * uu, z, cc)

    def at(d):
        return {"dp": d, "tensor": ten}

    def peer_u(k):
        return at(dev_uv(wrap(u + k), v, c))

    def peer_v(k):
        return at(dev_uv(u, wrap(v + k), c))

    peer_z = at(dev(x, y, oz, c))
    peer_w = {"dp": dev(x, y, oz, c), "tensor": wrap(ten + 3 + 2 * z)}
    peer_c = at(dev(x, y, z, oc))

    def pair_of(uu, vv):
        return (1 - c) * (uu * 4 + vv) + c * (vv * 4 + uu)

    sends, recvs = Sems(), Sems()

    def rcopy(src, dst, send_i, recv_i, to):
        return pltpu.make_async_remote_copy(
            src_ref=src, dst_ref=dst, send_sem=send_sem.at[send_i], recv_sem=recv_sem.at[recv_i],
            device_id=to, device_id_type=MESH,
        )

    def wait_sent(ref, send_i):
        rcopy(ref, ref, send_i, 0, peer_c).wait_send()

    def wait_got(ref, recv_i):
        rcopy(ref, ref, 0, recv_i, peer_c).wait_recv()

    def columns(p):
        return pl.ds(pl.multiple_of(p * 2 * BLK, 2 * BLK), 2 * BLK)

    def act_copy(i, p):
        return pltpu.make_async_copy(act_hbm.at[:, columns(p)], act.at[:, columns(p)], act_sem.at[i])

    def visit(i):
        g = wrap(x + wrap(lax.div(i, 4) + 1))
        j = wrap(y + wrap(lax.rem(i, 4) + 1))
        uu = (1 - c) * g + c * j
        vv = (1 - c) * j + c * g
        return g * 4 + j, uu, vv, wrap(uu - u + 4)

    def start_load(i, _):
        act_copy(i, visit(i)[0]).start()
        return 0

    lax.fori_loop(0, LOADS_FIRST, start_load, 0)
    barrier = pltpu.get_barrier_semaphore()

    def chip(n):
        if isinstance(n, int):
            dz, dx, dy = n // 16, n // 4 % 4, n % 4
        else:
            dz, dx, dy = lax.div(n, 16), lax.rem(lax.div(n, 4), 4), lax.rem(n, 4)
        xx, yy, zz = wrap(x + dx), wrap(y + dy), lax.rem(z + dz, 2)
        return xx, yy, zz, dz, dx, dy

    def chip_dev(n):
        xx, yy, zz, dz, dx, dy = chip(n)
        other = dz * ((dx + dy) % 2)
        return {"dp": dev(xx, yy, zz, c), "tensor": wrap(ten + other * (3 + 2 * z))}

    for n in range(31, 0, -1):
        pl.semaphore_signal(barrier, inc=1, device_id=chip_dev(n), device_id_type=MESH)
    for to in [peer_w, peer_c]:
        pl.semaphore_signal(barrier, inc=1, device_id=to, device_id_type=MESH)
    lax.fori_loop(LOADS_FIRST, 16, start_load, 0)
    cot_copy = pltpu.make_async_copy(cot_hbm, cot_ref, act_sem.at[16])
    cot_copy.start()


    r_i = lax.broadcasted_iota(jnp.int32, (S_DEV, S_DEV), 0)
    c_i = lax.broadcasted_iota(jnp.int32, (S_DEV, S_DEV), 1)
    rows = jnp.broadcast_to(rows_ref[...].astype(F32), (S_DEV, S_DEV))
    row_col = jnp.sum(jnp.where(r_i == c_i, rows, 0.0), axis=1, keepdims=True)
    tok = lax.broadcasted_iota(jnp.int32, onehot.shape, 1).astype(F32)
    onehot[...] = jnp.where(tok == row_col, 1.0, 0.0).astype(BF16)
    ss[32, :, :] = jnp.zeros((8, HALF), F32)

    pick_s, pick_r = sends(), recvs(4)
    pair_s, pair_r = sends(), recvs(16)
    zb_s, zb_r = sends(), recvs(2)
    rel_s, rel_r = sends(), recvs(4)
    rs1_s, rs1_r = sends(), recvs(8)
    rows2_s, rows2_r = sends(), recvs(4)
    g1_s, g1_r = sends(), recvs()
    g2_s, g2_r = sends(), recvs(4)
    rs2_s, rs2_r = sends(2), recvs(2)
    rs3_s, rs3_r = sends(), recvs()
    rs4_s, rs4_r = sends(), recvs()
    gx_s, gx_r = sends(3), recvs(3)
    gz_s, gz_r = sends(3), recvs(3)
    inv_s, inv_r = sends(2), recvs(2)
    s_s, s_r = sends(), recvs()
    t_s, t_r = sends(), recvs()
    out_s, out_r = sends(), recvs()
    assert sends.used <= SENDS and recvs.used <= RECVS

    def pick_copy(p, uu, vv, k):
        return rcopy(
            picks.at[:, p], r1.at[:, vv, k], pick_s, pick_r + vv, at(dev_uv(uu, v, c))
        )

    def pick_body(i, _):
        p = visit(i)[0]
        act_copy(i, p).wait()
        res = jnp.dot(onehot[...], act[:, columns(p)], preferred_element_type=F32).astype(BF16)
        for zz in range(2):
            picks[zz, p, :, :] = res[:, zz * BLK:(zz + 1) * BLK]
        return 0

    def pick_send(i, _):
        p, uu, vv, k = visit(i)

        @pl.when(k != 0)
        def _():
            pick_copy(p, uu, vv, k).start()

        @pl.when(k == 0)
        def _():
            r1[:, vv, 0, :, :] = picks[:, p, :, :]

        return 0

    def pick_both(i, _):
        pick_body(i, 0)
        return pick_send(i, 0)

    with jax.named_scope("picks"):
        lax.fori_loop(0, PICKS_FIRST, pick_body, 0)
    with jax.named_scope("barrier"):
        pl.semaphore_wait(barrier, 33)
    with jax.named_scope("picks2"):
        lax.fori_loop(0, PICKS_FIRST, pick_send, 0)
        lax.fori_loop(PICKS_FIRST, 16, pick_both, 0)
    cot_copy.wait()
    pg[...] = jnp.dot(onehot[...], cot_ref[...], preferred_element_type=F32).astype(BF16)

    def g1_copy(k):
        return rcopy(pg, g1.at[k], g1_s, g1_r, peer_u(k))

    for k in (2, 1, 3):
        g1_copy(k).start()
    cott[...] = cot_ref[...].T

    def grad_pair(i):
        code = jnp.int32(0)
        for n, (a, b) in enumerate(GRAD_ORDER):
            code = jnp.where(i == n, a * 4 + b, code)
        return wrap(x + lax.div(code, 4)) * 4 + wrap(y + lax.rem(code, 4))

    def pair_copy(i, p):
        return rcopy(buf.at[oc, p], pairs.at[p], pair_s, pair_r + i, peer_c)

    def grad_part(i):
        p = grad_pair(i)
        res = jnp.dot(cott[...], act[:, columns(p)], preferred_element_type=F32)
        for zz in range(2):
            other = lax.rem(zz + z, 2)
            main = pl.ds(pl.multiple_of(MAIN - MAIN * other, 8), MAIN)
            tail = pl.ds(pl.multiple_of(2 * MAIN + TAIL * other, 8), TAIL)
            for h in range(2):
                part = res[h * HALF:(h + 1) * HALF, zz * BLK:(zz + 1) * BLK]
                buf[h, p, main, :] = part[:MAIN]
                buf[h, p, tail, :] = part[MAIN:]
        pair_copy(i, p).start()

    def zb_copy(i, p, group):
        return rcopy(buf.at[c, p, SENT:], zb.at[i], zb_s, zb_r + group, peer_z)

    def pair_sum(i):
        p = grad_pair(i)
        pair_copy(i, p).wait_recv()
        buf[c, p, :, :] = buf[c, p, :, :] + pairs[p, :, :]
        @pl.when(i < 7)
        def _():
            zb_copy(i, p, 0).start()

        @pl.when(i >= 7)
        def _():
            zb_copy(i, p, 1).start()

    def early(i, _):
        grad_part(i)
        return 0

    def late(i, _):
        grad_part(i)
        pair_sum(i - LAG)
        return 0

    def rest(i, _):
        pair_sum(i)
        return 0

    def zb_add(i, _):
        p = grad_pair(i)
        buf[c, p, SENT - TAIL:SENT, :] = buf[c, p, SENT - TAIL:SENT, :] + zb[i, :, :]
        return 0

    UP, DOWN = (2, 1), (3, 0)

    def block(k, m):
        return buf.at[c, pair_of(wrap(u + k), wrap(v + m)), 0:SENT]

    def rel_copy(k, n):
        m = (UP if k == 1 else DOWN)[n]
        return rcopy(block(2, m), rel.at[k // 2, n], rel_s, rel_r + (k // 2) * 2 + n, peer_u(k))

    def rs1_copy(k, m):
        return rcopy(block(k, m), rs1.at[k // 2, m], rs1_s, rs1_r + (k // 2) * 4 + m, peer_u(k))

    with jax.named_scope("grad_a"):
        lax.fori_loop(0, LAG, early, 0)
        lax.fori_loop(LAG, GRAD_SPLIT, late, 0)

    def g2_copy(k):
        return rcopy(g1, g2.at[k], g2_s, g2_r + k, peer_v(k))

    def rows2_copy(k):
        return rcopy(r1.at[:, wrap(v + k)], r2.at[:, k], rows2_s, rows2_r + k, peer_v(k))

    with jax.named_scope("rows1wait"):
        for k in (2, 1, 3):
            wait_got(r1.at[:, wrap(v + k), 1:4], pick_r + wrap(v + k))
            rows2_copy(k).start()
        wait_got(g1.at[1:4], g1_r)
        g1[0, :, :] = pg[...]
        for k in (2, 1, 3):
            g2_copy(k).start()
        wait_got(r1.at[:, v, 1:4], pick_r + v)

    with jax.named_scope("grad_b"):
        lax.fori_loop(GRAD_SPLIT, 16, late, 0)
    with jax.named_scope("grad_c"):
        lax.fori_loop(16 - LAG, 16, rest, 0)
        wait_got(zb.at[0:7], zb_r)
        lax.fori_loop(0, 7, zb_add, 0)
    for n in range(2):
        for k in (1, 3):
            rel_copy(k, n).start()

    def gx_copy(n):
        return rcopy(gr.at[n], gx.at[n], gx_s + n, gx_r + n, peer_c)

    with jax.named_scope("rows2wait"):
        for zz in range(2):
            gr[zz, :, :] = gram(r1[zz, v, :, :, :].reshape(4 * S_DEV, BLK))
        gr[2, :, :] = gram(g1[...].reshape(4 * S_DEV, BLK))
        for k in (1, 3, 2):
            rows2_copy(k).wait_recv()
            for zz in range(2):
                gr[zz, :, :] += gram(r2[zz, k, :, :, :].reshape(4 * S_DEV, BLK))

    @pl.when(c == 1)
    def _():
        gx_copy(oz).start()
        gx_copy(z).start()

    wait_got(zb.at[7:16], zb_r + 1)
    lax.fori_loop(7, 16, zb_add, 0)
    for n in range(2):
        rs1_copy(1, DOWN[n]).start()
        rs1_copy(3, UP[n]).start()

    def gz_copy(n):
        half = pl.ds(n * HALF, HALF)
        return rcopy(gh.at[half], gz.at[half], gz_s + n, gz_r + n, peer_w if n else peer_z)

    gz_all = rcopy(gh, gz, gz_s + 2, gz_r + 2, peer_z)

    @pl.when(c == 0)
    def _():
        with jax.named_scope("gx"):
            gx_copy(oz).wait_recv()
        gh[...] = gr[oz, :, :] + gx[oz, :, :]
        gz_copy(0).start()
        gz_copy(1).start()
        gx_copy(z).wait_recv()
        m_ref[...] = gr[z, :, :] + gx[z, :, :]

    def fill_table(i, _):
        xx, yy, zz, _, _, _ = chip(lax.div(i, 2))
        d = dev(xx, yy, zz, lax.rem(i, 2))
        b = jnp.int32(-1)
        for q in range(32):
            b = jnp.where(owner_ref[q] == d, q, b)
        bb = jnp.maximum(b, 0)
        bz = lax.rem(bb + z, 2)
        by = wrap(y - lax.rem(lax.div(bb, 2), 4) + 4)
        bx = wrap(x - lax.div(bb, 8) + 4)
        table[i] = jnp.where(b < 0, 32, bz * 16 + bx * 4 + by)
        return 0

    with jax.named_scope("table"):
        lax.fori_loop(0, 64, fill_table, 0)

    with jax.named_scope("g2wait"):
        for k in (1, 3, 2):
            g2_copy(k).wait_recv()
            gr[2, :, :] += gram(g2[k, :, :, :].reshape(4 * S_DEV, BLK))

    @pl.when(c == 0)
    def _():
        gx_copy(2).start()

    @pl.when(c == 1)
    def _():
        with jax.named_scope("gxg"):
            gx_copy(2).wait_recv()
        gh[...] = gr[2, :, :] + gx[2, :, :]
        gz_all.start()
        m_ref[...] = gh[...]

    def relay():
        with jax.named_scope("relay"):
            for n in range(2):
                for k in (1, 3):
                    rel_copy(k, n).wait_recv()
                    m = (UP if k == 1 else DOWN)[n]
                    p = pair_of(wrap(u + k), wrap(v + m))
                    buf[c, p, 0:SENT, :] = buf[c, p, 0:SENT, :] + rel[k // 2, n, :, :]
                    rs1_copy(k, m).start()

    relay()

    def factor(scale):
        m_ref[...] = (m_ref[...] + gz[...]) * scale + DAMPING * eye(BLK)

    def core1_factor():
        with jax.named_scope("gz"):
            gz_all.wait_recv()
        factor(12.0)

    def s_copy(n):
        xx, yy, zz, dz, dx, dy = chip(n)
        return rcopy(isl.at[zz, xx * 4 + yy], ss.at[n], s_s, s_r, chip_dev(n))

    def s_start():
        for n in range(31, 0, -1):
            s_copy(n).start()

    def rs2_copy(k, part):
        rows = pl.ds(MAIN, HALF) if part else pl.ds(0, MAIN)
        to = rs2b if part else rs2a
        return rcopy(acc1.at[k, rows], to.at[k], rs2_s + part, rs2_r + part, peer_v(k))

    def rs1_finish():
        with jax.named_scope("rs1"):
            for m in (3, 2, 1, 0):
                wait_got(rs1.at[0, m], rs1_r + m)
                wait_got(rs1.at[1, m], rs1_r + 4 + m)
                acc1[m, :, :] = block(0, m)[...] + rs1[0, m, :, :] + rs1[1, m, :, :]
                if m:
                    rs2_copy(m, 0).start()
            for m in (3, 2, 1):
                rs2_copy(m, 1).start()

    half_copy = rcopy(isx, isl, inv_s, inv_r, peer_c)
    ginv_copy = rcopy(x_ref, ginv, inv_s + 1, inv_r + 1, peer_c)

    def t_copy(n):
        return rcopy(dd.at[n], tt.at[n], t_s, t_r, chip_dev(n))

    def slots_back():
        ss[0, :, :] = isl[z, x * 4 + y, :, :]
        with jax.named_scope("s"):
            wait_got(ss.at[1:32], s_r)
        with jax.named_scope("select"):
            for n in range(31, -1, -1):
                for cc in range(2):
                    dd[n, cc, :, :] = ss[table[2 * n + cc], :, :]
                if n:
                    t_copy(n).start()
        tt[0, :, :, :] = dd[0, :, :, :]

    @pl.when(c == 0)
    def _():
        with jax.named_scope("gz"):
            gz_copy(0).wait_recv()
            gz_copy(1).wait_recv()
        factor(1.0 / 4096.0)
        with jax.named_scope("newton_begin"):
            newton_begin(m_ref, x_ref, e_ref)
        with jax.named_scope("newton_end"):
            newton_end(x_ref, e_ref)
        for zz in range(2):
            cols = pl.ds(zz * HALF, HALF)
            isx[zz, :, :, :] = x_ref[HALF:, cols].reshape(16, 8, HALF)
            isl[zz, :, :, :] = x_ref[:HALF, cols].reshape(16, 8, HALF)
        half_copy.start()
        s_start()
        rs1_finish()
        slots_back()

    @pl.when(c == 1)
    def _():
        core1_factor()
        with jax.named_scope("newton_begin"):
            newton_begin(m_ref, x_ref, e_ref)
        with jax.named_scope("half"):
            half_copy.wait_recv()
        s_start()
        rs1_finish()
        slots_back()

    with jax.named_scope("drain"):
        wait_sent(picks.at[:, 0:12], pick_s)
        wait_sent(buf.at[oc], pair_s)
        wait_sent(zb, zb_s)
        wait_sent(g1.at[1:4], g1_s)
        wait_sent(g2.at[1:4], g2_s)
        wait_sent(r2.at[:, 1:4], rows2_s)
        wait_sent(rel, rel_s)
        wait_sent(rs1, rs1_s)

        @pl.when(c == 0)
        def _():
            for copy in [gx_copy(2), gz_copy(0), gz_copy(1), half_copy]:
                copy.wait_send()

        @pl.when(c == 1)
        def _():
            for copy in [gx_copy(oz), gx_copy(z), gz_all]:
                copy.wait_send()

    with jax.named_scope("rs2a"):
        wait_got(rs2a.at[1:4], rs2_r)
    acc2[...] = acc1[0, 0:MAIN, :] + rs2a[1, :, :] + rs2a[2, :, :] + rs2a[3, :, :]
    rs3_copy = rcopy(acc2, rs3, rs3_s, rs3_r, peer_z)
    rs3_copy.start()

    @pl.when(c == 1)
    def _():
        with jax.named_scope("newton_end"):
            newton_end(x_ref, e_ref)
        ginv_copy.start()

    with jax.named_scope("rs2b"):
        wait_got(rs2b.at[1:4], rs2_r + 1)
    fin[c, :, :] = acc1[0, MAIN:SENT, :] + rs2b[1, :, :] + rs2b[2, :, :] + rs2b[3, :, :]
    with jax.named_scope("rs3"):
        rs3_copy.wait_recv()
    fin[c, 0:MAIN, :] = fin[c, 0:MAIN, :] + rs3[...]
    rs4_copy = rcopy(fin.at[c], fin.at[c], rs4_s, rs4_r, peer_c)
    rs4_copy.start()

    def assemble(n, _):
        dz, dx, dy = lax.div(n, 16), lax.rem(lax.div(n, 4), 4), lax.rem(n, 4)
        row = wrap(x - dx + 4) * 4 + wrap(y - dy + 4)
        zz = lax.rem(z + dz, 2)
        for cc in range(2):
            outh[cc, 0, zz, row, :, :] = tt[n, cc, :, :]
        return 0

    with jax.named_scope("t"):
        wait_got(tt.at[1:32], t_r)
    lax.fori_loop(0, 32, assemble, 0, unroll=4)
    out_copy = rcopy(outh.at[oc, 0], outh.at[oc, 1], out_s, out_r, peer_c)
    out_copy.start()

    with jax.named_scope("rs4"):
        rs4_copy.wait_recv()

    @pl.when(c == 0)
    def _():
        ginv_copy.wait_recv()

    @pl.when(c == 1)
    def _():
        ginv[...] = x_ref[...]

    with jax.named_scope("final"):
        grad = fin[...].reshape(BLK, BLK)
        nt = (((1,), (1,)), ((), ()))
        left = dot_hi(isl[0, :, :, :].reshape(HALF, HALF), grad[:, :HALF], nt)
        left += dot_hi(isl[1, :, :, :].reshape(HALF, HALF), grad[:, HALF:], nt)
        step_v[...] = dot_hi(left, ginv[...])
    step_copy = pltpu.make_async_copy(step_v, step_hbm, out_sem.at[0])
    step_copy.start()

    with jax.named_scope("outx"):
        out_copy.wait_recv()
    for n in range(2):
        h = (1 - n) * c + n * oc
        for zz in range(2):
            slot_v[h, :, zz * HALF:(zz + 1) * HALF] = outh[c, n, zz, :, :, :].reshape(HALF, HALF)
    slot_copy = pltpu.make_async_copy(slot_v, slot_hbm, out_sem.at[1])
    slot_copy.start()

    with jax.named_scope("drain2"):
        wait_sent(ss.at[1:32], s_s)
        wait_sent(tt.at[1:32], t_s)
        wait_sent(rs2a.at[1:4], rs2_s)
        wait_sent(rs2b.at[1:4], rs2_s + 1)
        for copy in [rs3_copy, rs4_copy, out_copy]:
            copy.wait_send()

        @pl.when(c == 1)
        def _():
            ginv_copy.wait_send()

    with jax.named_scope("store"):
        step_copy.wait()
        slot_copy.wait()


def settle(step_in, slot_in, step_out, slot_out):
    step_out[...] = step_in[...]
    slot_out[...] = slot_in[...]


def per_device(activations, cotangent, sampled_rows, block_owner):
    tokens, width = activations.shape
    vmem = pltpu.VMEM
    step, slot = pl.pallas_call(
        kernel,
        out_shape=(
            jax.ShapeDtypeStruct((HALF, BLK), F32),
            jax.ShapeDtypeStruct((2, HALF, BLK), F32),
        ),
        in_specs=[
            pl.BlockSpec(memory_space=pl.ANY),
            pl.BlockSpec(memory_space=pl.ANY),
            pl.BlockSpec(memory_space=pltpu.VMEM),
            pl.BlockSpec(memory_space=pltpu.SMEM),
        ],
        out_specs=(
            pl.BlockSpec(memory_space=pl.ANY),
            pl.BlockSpec(memory_space=pl.ANY),
        ),
        scratch_shapes=[
            vmem((tokens, width), BF16),
            vmem((tokens, BLK), BF16),
            vmem((BLK, tokens), BF16),
            vmem((S_DEV, tokens), BF16),
            vmem((2, 16, BLK, BLK), F32),
            vmem((16, BLK, BLK), F32),
            vmem((16, TAIL, BLK), F32),
            vmem((2, 2, SENT, BLK), F32),
            vmem((2, 4, SENT, BLK), F32),
            vmem((4, SENT, BLK), F32),
            vmem((4, MAIN, BLK), F32),
            vmem((4, HALF, BLK), F32),
            vmem((MAIN, BLK), F32),
            vmem((MAIN, BLK), F32),
            vmem((2, HALF, BLK), F32),
            vmem((2, 16, S_DEV, BLK), BF16),
            vmem((S_DEV, BLK), BF16),
            vmem((2, 4, 4, S_DEV, BLK), BF16),
            vmem((2, 4, 4, S_DEV, BLK), BF16),
            vmem((4, S_DEV, BLK), BF16),
            vmem((4, 4, S_DEV, BLK), BF16),
            vmem((3, BLK, BLK), F32),
            vmem((3, BLK, BLK), F32),
            vmem((BLK, BLK), F32),
            vmem((BLK, BLK), F32),
            vmem((BLK, BLK), F32),
            vmem((BLK, BLK), F32),
            vmem((BLK, BLK), F32),
            vmem((2, 16, 8, HALF), F32),
            vmem((2, 16, 8, HALF), F32),
            vmem((BLK, BLK), F32),
            vmem((33, 8, HALF), F32),
            vmem((32, 2, 8, HALF), F32),
            vmem((32, 2, 8, HALF), F32),
            vmem((2, 2, 2, 16, 8, HALF), F32),
            vmem((2, HALF, BLK), F32),
            vmem((HALF, BLK), F32),
            pltpu.SMEM((64,), jnp.int32),
            pltpu.SemaphoreType.DMA((17,)),
            pltpu.SemaphoreType.DMA((2,)),
            pltpu.SemaphoreType.DMA((SENDS,)),
            pltpu.SemaphoreType.DMA((RECVS,)),
        ],
        compiler_params=pltpu.CompilerParams(
            collective_id=0, has_side_effects=True, vmem_limit_bytes=60 * 1024 * 1024
        ),
    )(activations, cotangent, sampled_rows.reshape(1, S_DEV), block_owner)
    step, slot = pl.pallas_call(
        settle,
        out_shape=(
            jax.ShapeDtypeStruct((HALF, BLK), F32),
            jax.ShapeDtypeStruct((2, HALF, BLK), F32),
        ),
    )(step, slot)
    return step, slot.reshape(1, BLK, BLK)


def solution(mesh):
    return jax.shard_map(
        per_device,
        mesh=mesh,
        in_specs=(P("dp", None), P("dp", "tensor"), P("dp"), P()),
        out_specs=(P("dp", "tensor"), P("dp", None, None)),
        check_vma=False,
    )
```
